256 devices in a mesh: dp: 32 (over y, z_lo, core), seq: 8 (over z_hi, x).
Axes of the slice: x: 4, y: 4, z: 8 (z_hi: 2, z_lo: 4; z = z_hi * 4 + z_lo), core: 2. Of those that a mesh axis runs over, the one named last changes fastest.
Arguments:
- stream_in: bfloat16 [32, 1024, 768], P('dp', 'seq'), may hold values from -30 to 30
- queries: bfloat16 [32, 1024, 768], P('dp', 'seq'), may hold values from -5.6 to 5.6
- key_rows: bfloat16 [32, 1024, 768], P('dp', 'seq'), may hold values from -5.6 to 5.6
- value_rows: bfloat16 [32, 1024, 768], P('dp', 'seq'), may hold values from -6 to 6
- conv_weight: bfloat16 [768, 5, 768], P('dp'), may hold values from -0.09375 to 0.09375
- cotangent: bfloat16 [32, 1024, 768], P('dp', 'seq'), may hold values from -6 to 6
Outputs:
- grad_stream: bfloat16 [32, 1024, 768], P('dp', 'seq')
- grad_queries: bfloat16 [32, 1024, 768], P('dp', 'seq')
- grad_keys: bfloat16 [32, 1024, 768], P('dp', 'seq')
- grad_values: bfloat16 [32, 1024, 768], P('dp', 'seq')
- grad_weight: float32 [768, 5, 768], P('dp')
The draws below stay inside these ranges and needn't reach their ends.
All inputs are finite; a program needn't handle non-finite values.
Results may differ from the reference program's by a relative error of at most 0.017.
Values may be sent and summed in bfloat16 or wider, within the bound.
A program may use at most 128 MiB of HBM per device.

```python
import jax
import jax.numpy as jnp
from jax import lax

HEADS = 8
HEAD_DIM = 96
CH = 768
TAPS = 5
ROWS = 128
L = 1024
BATCH = 32


def draw_queries(key, part):
    base_key = jax.random.fold_in(key, 1)
    return jnp.clip(jax.random.normal(base_key, (BATCH, L, CH), jnp.float32), -5.0, 5.0).astype(jnp.bfloat16)


def draw_key_rows(key, part):
    base_key = jax.random.fold_in(key, 2)
    return jnp.clip(jax.random.normal(base_key, (BATCH, L, CH), jnp.float32), -5.0, 5.0).astype(jnp.bfloat16)


def draw_stream_in(key, part):
    row_spread = 0.35
    col_spread = 1.1513
    row_scale = jnp.exp(jax.random.uniform(jax.random.fold_in(key, 3), (BATCH, L, 1), jnp.float32, -row_spread, row_spread))
    col_scale = jnp.exp(jax.random.uniform(jax.random.fold_in(key, 4), (CH,), jnp.float32, -col_spread, col_spread))
    base_key = jax.random.fold_in(key, 5)
    values = jnp.clip(jax.random.normal(base_key, (BATCH, L, CH), jnp.float32), -6.0, 6.0)
    return (values * row_scale * col_scale[None, None, :]).astype(jnp.bfloat16)


def spiked(entries, key, source, target, blocks, factor):
    owner, partner = [(jnp.arange(entries.shape[dim]) // (entries.shape[dim] // blocks)).reshape([-1 if axis == dim else 1 for axis in range(entries.ndim)]) for dim in (source, target)]
    chosen = jax.random.permutation(key, blocks)[partner]
    strong = (owner == chosen) | (owner == (partner + blocks // 2) % blocks)
    return jnp.where(strong, factor * entries, entries)


def level_of(own_key, dims, cuts, least, top_value):
    def one(dim, shards_of):
        heights = jax.random.uniform(jax.random.fold_in(jax.random.fold_in(own_key, 6), dim), (shards_of,), jnp.float32, least / len(cuts), top_value / len(cuts))
        return jnp.repeat(jnp.exp(heights), dims[dim] // shards_of).reshape((-1,) + (1,) * (len(dims) - dim - 1))

    factor_of = one(*cuts[0])
    for cut in cuts[1:]:
        factor_of = factor_of * one(*cut)
    return factor_of


def normal_values(key, extent, width, reach, shards=(), held_as=jnp.bfloat16):
    array = width * jax.random.normal(key, extent, jnp.float32)
    if shards:
        array = array * level_of(key, extent, shards, -0.22, 0.18)
    return jnp.clip(array, -reach, reach).astype(held_as)


def noise_with(rng, shape, deviation, most, pieces, heavy, dtype=jnp.bfloat16):
    values = deviation * jax.random.normal(rng, shape, jnp.float32)
    if pieces:
        values = values * level_of(rng, shape, pieces, -0.22, 0.18)
    return jnp.clip(spiked(values, jax.random.fold_in(rng, 3), *heavy), -most, most).astype(dtype)


def setup_inputs(seed: int = 0) -> dict:
    streams_of = jax.random.split(jax.random.key(seed), 7)
    stream_in = draw_stream_in(jax.random.fold_in(streams_of[6], 71), 0)
    queries = draw_queries(jax.random.fold_in(streams_of[6], 71), 0)
    key_rows = draw_key_rows(jax.random.fold_in(streams_of[6], 71), 0)
    value_rows = normal_values(streams_of[3], (BATCH, L, CH), 1.0, 6.0, ((0, 32), (1, 8)))
    conv_weight = normal_values(streams_of[4], (CH, TAPS, CH), (TAPS * CH) ** -0.5, 0.09375, ((0, 32),))
    cotangent = noise_with(streams_of[5], (BATCH, L, CH), 1.0, 6.0, ((0, 32), (1, 8)), (0, 2, 32, 2.75))
    return {"stream_in": stream_in, "queries": queries, "key_rows": key_rows, "value_rows": value_rows, "conv_weight": conv_weight, "cotangent": cotangent}


def activate(stream):
    values = stream.astype(jnp.float32)
    square = lax.optimization_barrier(jnp.mean(values * values, axis=-1, keepdims=True))
    return jax.nn.gelu(values * lax.rsqrt(square + 1e-06), approximate=True)

def one_sequence(stream_in, queries, key_rows, value_rows, cotangent, conv_weight):
    scale = HEAD_DIM ** (-0.5)
    half = TAPS // 2
    qf = queries.astype(jnp.float32).reshape(L, HEADS, HEAD_DIM)
    kf = key_rows.astype(jnp.float32).reshape(L, HEADS, HEAD_DIM)
    vf = value_rows.astype(jnp.float32).reshape(L, HEADS, HEAD_DIM)
    scores = jnp.einsum('ihd,jhd->hij', qf, kf) * scale
    top = lax.optimization_barrier(jnp.max(scores, axis=-1, keepdims=True))
    expo = jnp.exp(scores - top)
    total = lax.optimization_barrier(jnp.sum(expo, axis=-1, keepdims=True))
    expo_b = expo.astype(jnp.bfloat16).astype(jnp.float32)
    attended = jnp.einsum('hij,jhd->ihd', expo_b, vf) / jnp.transpose(total, (1, 0, 2))
    stream = (stream_in.astype(jnp.float32) + attended.reshape(L, CH)).astype(jnp.bfloat16)
    hidden, pullback = jax.vjp(activate, stream.astype(jnp.float32))
    hidden_b = hidden.astype(jnp.bfloat16)
    hid_pad = jnp.pad(hidden_b, ((half, half), (0, 0)))
    cot_pad = jnp.pad(cotangent, ((half, half), (0, 0)))
    windows = jnp.stack([hid_pad[tap:tap + L] for tap in range(TAPS)], axis=1).reshape(L, TAPS * CH)
    weight_term = jnp.einsum('to,tk->ok', cotangent.astype(jnp.float32), windows.astype(jnp.float32))
    back = jnp.zeros((L, CH), jnp.float32)
    for tap in range(TAPS):
        start = 2 * half - tap
        back = back + jnp.dot(cot_pad[start:start + L], conv_weight[:, tap, :], preferred_element_type=jnp.float32)
    grad_stream = (cotangent.astype(jnp.float32) + pullback(back)[0]).astype(jnp.bfloat16)
    dout = grad_stream.astype(jnp.float32).reshape(L, HEADS, HEAD_DIM)
    probs = expo / total
    probs_b = probs.astype(jnp.bfloat16).astype(jnp.float32)
    delta = jnp.transpose(lax.optimization_barrier(jnp.sum(dout * attended, axis=-1)), (1, 0))[:, :, None]
    dprob = jnp.einsum('ihd,jhd->hij', dout, vf)
    dscore = (probs * (dprob - delta)).astype(jnp.bfloat16).astype(jnp.float32)
    grad_queries = (jnp.einsum('hij,jhd->ihd', dscore, kf) * scale).reshape(L, CH).astype(jnp.bfloat16)
    blocks = L // ROWS
    ds_blocks = dscore.reshape(HEADS, blocks, ROWS, L)
    pb_blocks = probs_b.reshape(HEADS, blocks, ROWS, L)
    q_blocks = qf.reshape(blocks, ROWS, HEADS, HEAD_DIM)
    o_blocks = dout.reshape(blocks, ROWS, HEADS, HEAD_DIM)
    dk_parts = (jnp.einsum('hbij,bihd->bjhd', ds_blocks, q_blocks) * scale).astype(jnp.bfloat16)
    dv_parts = jnp.einsum('hbij,bihd->bjhd', pb_blocks, o_blocks).astype(jnp.bfloat16)
    grad_keys = lax.optimization_barrier(jnp.sum(dk_parts.astype(jnp.float32), axis=0)).reshape(L, CH).astype(jnp.bfloat16)
    grad_values = lax.optimization_barrier(jnp.sum(dv_parts.astype(jnp.float32), axis=0)).reshape(L, CH).astype(jnp.bfloat16)
    return (grad_stream, grad_queries, grad_keys, grad_values, weight_term)

def reference(stream_in, queries, key_rows, value_rows, conv_weight, cotangent):

    def step(carry, items):
        outs = one_sequence(items[0], items[1], items[2], items[3], items[4], conv_weight)
        return (carry + outs[4], outs[:4])
    start = jnp.zeros((CH, TAPS * CH), jnp.float32)
    summed, stacked = lax.scan(step, start, (stream_in, queries, key_rows, value_rows, cotangent))
    grad_weight = (summed / jnp.sqrt(jnp.float32(BATCH * L))).reshape(CH, TAPS, CH)
    return (stacked[0], stacked[1], stacked[2], stacked[3], grad_weight)
```

```python
import jax
import jax.numpy as jnp
from jax import lax
from jax.experimental import pallas as pl
from jax.experimental.pallas import tpu as pltpu
from jax.sharding import PartitionSpec as P

HEADS = 8
HD = 96
TAPS = 5
ROWS = 128
CH = 768
QC = 192
W5 = TAPS * QC
EXT = 640
MESH = pl.DeviceIdType.MESH
F32 = jnp.float32
BF = jnp.bfloat16
NT = (((1,), (1,)), ((), ()))
SCALE = HD ** (-0.5)
LOG2E = 1.4426950408889634
GC = 0.7978845608028654
GA = 0.044715


def dot(a, b):
    return jnp.dot(a, b, preferred_element_type=F32)


def dot_nt(a, b):
    return lax.dot_general(a, b, NT, preferred_element_type=F32)


def lanes(parts):
    return jnp.concatenate(parts, axis=1)


def tr(value):
    return value.astype(F32).T


def copy_to(src, dst, send, recv, dev):
    return pltpu.make_async_remote_copy(
        src_ref=src, dst_ref=dst, send_sem=send, recv_sem=recv, device_id=dev, device_id_type=MESH
    )


def kernel(
    x_ref, q_ref, k_ref, v_ref, w_ref, c_ref,
    gs_out, dq_out, dk_out, dv_out, gw_out,
    qkv_s, qkv_r, kn, vn, st, ex, itot, attf, att_s, att_r,
    cblk, hal, cfull, coth, wbuf, wt, bk_s, bk_r, h_s, h_r, hw,
    gs_s, gs_r, dqa, d_s, d_r, gp, yb, zs, zb, ms, mb, fs, ob, strm,
    qkv_ss, qkv_rs, att_ss, att_rs, gs_ss, gs_rs, d_ss, d_rs,
    c_ss, c_rs, hal_ss, hal_rs, co_ss, co_rs,
    wy_ss, wy_rs, wz_ss, wz_rs, wc_ss, wc_rs,
    bk_ss, bk_rs, h_ss, h_rs, y_ss, y_rs, z_ss, z_rs, m_ss, m_rs, f_ss, f_rs,
):
    me = lax.axis_index("seq")
    dd = lax.axis_index("dp")
    zh = lax.div(me, 4)
    x = lax.rem(me, 4)
    y = lax.div(dd, 8)
    zl = lax.rem(lax.div(dd, 2), 4)
    c = lax.rem(dd, 2)
    oc = 1 - c
    z = zh * 4 + zl
    odp = y * 8 + zl * 2 + oc

    def seq_dev(p):
        return {"seq": p, "dp": dd}

    def xc_dev(xx, cc):
        return {"seq": zh * 4 + xx, "dp": y * 8 + zl * 2 + cc}

    def y_dev(yy):
        return {"seq": me, "dp": yy * 8 + zl * 2 + c}

    def z_dev(step):
        zz = lax.rem(z + step + 8, 8)
        return {"seq": lax.div(zz, 4) * 4 + x, "dp": y * 8 + lax.rem(zz, 4) * 2 + c}

    def loop(lo, hi, fn):
        def step(i, carry):
            fn(i)
            return carry

        lax.fori_loop(lo, hi, step, 0)

    hal[...] = jnp.zeros_like(hal)
    barrier = pltpu.get_barrier_semaphore()

    def hello(dev):
        pl.semaphore_signal(barrier, inc=1, device_id=dev, device_id_type=MESH)

    loop(1, 8, lambda r: hello(seq_dev(lax.rem(me + r, 8))))
    loop(0, 4, lambda xx: hello(xc_dev(xx, oc)))
    loop(1, 4, lambda r: hello(y_dev(lax.rem(y + r, 4))))
    for step in (1, -1, 2, -2):
        hello(z_dev(step))

    qkv_s[0] = tr(k_ref[...]).astype(BF).reshape(8, HD, ROWS)
    qkv_s[1] = tr(q_ref[...]).astype(BF).reshape(8, HD, ROWS)
    qkv_s[2] = tr(v_ref[...]).astype(BF).reshape(8, HD, ROWS)
    cblk[x] = tr(c_ref[...]).astype(BF)
    wbuf[c, zl, y] = w_ref[...]
    pl.semaphore_wait(barrier, 18)

    def exch(src, dst, ssem, rsem, p):
        return copy_to(src.at[p], dst.at[me], ssem.at[p], rsem.at[me], seq_dev(p))

    def exch_recv(src, dst, ssem, rsem, p):
        return copy_to(src.at[p], dst.at[p], ssem.at[p], rsem.at[p], seq_dev(p))

    def start_all(src, dst, ssem, rsem):
        loop(1, 8, lambda r: exch(src, dst, ssem, rsem, lax.rem(me + r, 8)).start())

    def recv_all(src, dst, ssem, rsem):
        loop(1, 8, lambda r: exch_recv(src, dst, ssem, rsem, lax.rem(me + r, 8)).wait_recv())

    def sent_all(src, dst, ssem, rsem):
        loop(1, 8, lambda r: exch_recv(src, dst, ssem, rsem, lax.rem(me + r, 8)).wait_send())

    def qkv(t):
        return qkv_s.at[t], qkv_r.at[t], qkv_ss.at[t], qkv_rs.at[t]

    for t in range(3):
        start_all(*qkv(t))

    def wy(yy, slot):
        return copy_to(wbuf.at[c, zl, slot], wbuf.at[c, zl, slot], wy_ss.at[yy], wy_rs.at[slot], y_dev(yy))

    loop(1, 4, lambda r: wy(lax.rem(y + r, 4), y).start())

    def cx(xx, slot):
        return copy_to(cblk.at[slot], cblk.at[slot], c_ss.at[xx], c_rs.at[slot], xc_dev(xx, c))

    loop(1, 4, lambda r: cx(lax.rem(x + r, 4), x).start())

    def edge(p, lo):
        rows = pl.ds(lo, 16)

        return copy_to(c_ref.at[rows], hal.at[pl.ds(lo, 16)], hal_ss.at[lax.rem(p, 4)], hal_rs, seq_dev(p))

    first = jnp.logical_and(zh == 1, x == 0)
    last = jnp.logical_and(zh == 0, x == 3)

    @pl.when(first)
    def _():
        loop(0, 4, lambda p: edge(p, 0).start())

    @pl.when(last)
    def _():
        loop(4, 8, lambda p: edge(p, 112).start())

    for t in range(3):
        qkv_r[t, me] = qkv_s[t, me]
    recv_all(*qkv(0))
    for b in range(8):
        kn[128 * b : 128 * b + 128, :] = tr(qkv_r[0, b]).astype(BF)
    recv_all(*qkv(1))

    loop(1, 4, lambda r: wy(lax.rem(y + r, 4), lax.rem(y + r, 4)).wait_recv())
    far = 2 - 4 * c

    def wz(i, step, slot):
        return copy_to(wbuf.at[c, slot], wbuf.at[c, slot], wz_ss.at[i], wz_rs.at[i], z_dev(step))

    wz(0, 1, zl).start()
    wz(1, -1, zl).start()
    wz(2, far, zl).start()

    recv_all(*qkv(2))
    for b in range(8):
        vn[128 * b : 128 * b + 128, :] = tr(qkv_r[2, b]).astype(BF)

    def pair(ref, t, i):
        return lanes([ref[t, 2 * i], ref[t, 2 * i + 1]])

    def forward(ib):
        qb = lanes([qkv_r[1, 2 * ib], qkv_r[1, 2 * ib + 1]])
        top = None
        for jb in range(4):
            s = dot(kn[256 * jb : 256 * jb + 256, :], qb)
            st[256 * jb : 256 * jb + 256, :] = s
            m = jnp.max(s, axis=0, keepdims=True)
            top = m if top is None else jnp.maximum(top, m)
        tot = jnp.zeros((1, 256), F32)
        acc = jnp.zeros((HD, 256), F32)
        for jb in range(4):
            e = jnp.exp2((st[256 * jb : 256 * jb + 256, :] - top) * (SCALE * LOG2E))
            ex[ib, 256 * jb : 256 * jb + 256, :] = e
            tot = tot + jnp.sum(e, axis=0, keepdims=True)
            acc = acc + dot(pair(qkv_r, 2, jb), e.astype(BF))
        inv = 1.0 / tot
        itot[ib] = inv
        att = acc * inv
        attf[ib] = att
        ab = att.astype(BF)
        for half in range(2):
            p = 2 * ib + half
            att_s[p] = ab[:, 128 * half : 128 * half + 128]

            @pl.when(p != me)
            def _():
                exch(att_s, att_r, att_ss, att_rs, p).start()

            @pl.when(p == me)
            def _():
                att_r[me] = att_s[me]

    loop(0, 4, forward)

    def wz_recv(i, step):
        slot = lax.rem(zl + step + 4, 4)
        return copy_to(wbuf.at[c, slot], wbuf.at[c, slot], wz_ss.at[i], wz_rs.at[i], z_dev(step))

    wz_recv(0, -1).wait_recv()
    wz_recv(1, 1).wait_recv()
    wz_recv(2, -far).wait_recv()

    def wc(slot):
        return copy_to(wbuf.at[slot], wbuf.at[slot], wc_ss, wc_rs, xc_dev(x, oc))

    wc(c).start()

    loop(1, 4, lambda r: cx(lax.rem(x + r, 4), lax.rem(x + r, 4)).wait_recv())

    @pl.when(zh == 0)
    def _():
        edge(0, 0).wait_recv()

    @pl.when(zh == 1)
    def _():
        edge(0, 112).wait_recv()

    halt = tr(hal[...]).astype(BF)
    for cc in range(2):
        for yy in range(4):
            lo = 192 * yy + 96 * cc
            for b in range(4):
                cfull[cc, yy, :, 128 * b : 128 * b + 128] = cblk[b, lo : lo + 96, :]
            cfull[cc, yy, :, 512:640] = halt[lo : lo + 96, :]

    co = copy_to(cfull.at[oc], coth, co_ss, co_rs, xc_dev(x, oc))
    co.start()

    wc(oc).wait_recv()
    for n in range(8):
        width = min(128, W5 - 128 * n)
        rows = []
        for cc in range(2):
            for yy in range(4):
                for j in range(4):
                    rows.append(wbuf[j % 2, 2 * cc + j // 2, yy, :, 128 * n : 128 * n + width].astype(F32))
        wt[128 * n : 128 * n + width, :] = jnp.concatenate(rows, axis=0).T.astype(BF)

    cot_all = cfull[...].reshape(CH, EXT)
    back_q = None
    for a in range(TAPS):
        part = dot(wt[QC * a : QC * a + QC, :], cot_all)
        shift = (a - 2) % EXT
        if shift:
            part = pltpu.roll(part, shift, 1)
        back_q = part if back_q is None else back_q + part
    back_b = back_q.astype(BF)
    for b in range(4):
        bk_s[b] = back_b[:, 128 * b : 128 * b + 128]
    bk_r[x] = bk_s[x]

    def bk(xx, slot_from, slot_to):
        return copy_to(bk_s.at[slot_from], bk_r.at[slot_to], bk_ss.at[xx], bk_rs.at[slot_to], xc_dev(xx, c))

    def bk_start(r):
        xx = lax.rem(x + r, 4)
        bk(xx, xx, x).start()

    def bk_wait(r):
        xx = lax.rem(x + r, 4)
        bk(xx, xx, xx).wait_recv()

    loop(1, 4, bk_start)

    xt = tr(x_ref[...])
    recv_all(att_s, att_r, att_ss, att_rs)
    u = (xt + att_r[...].astype(F32).reshape(CH, ROWS)).astype(BF).astype(F32)
    rs = lax.rsqrt(jnp.mean(u * u, axis=0, keepdims=True) + 1e-6)
    nn = u * rs
    th = jnp.tanh(GC * (nn + GA * (nn * nn * nn)))
    hid = (0.5 * nn * (1.0 + th)).astype(BF)
    h_s[...] = hid.reshape(4, QC, ROWS)
    h_r[c, x] = h_s[x]

    def hx(xx, cc):
        return copy_to(h_s.at[xx], h_r.at[c, x], h_ss.at[cc, xx], h_rs.at[c, x], xc_dev(xx, cc))

    def hx_recv(xx, cc):
        return copy_to(h_s.at[xx], h_r.at[cc, xx], h_ss.at[cc, xx], h_rs.at[cc, xx], xc_dev(xx, cc))

    loop(0, 4, lambda xx: hx(xx, oc).start())
    loop(1, 4, lambda r: hx(lax.rem(x + r, 4), c).start())

    loop(1, 4, bk_wait)
    bk_all = bk_r[...].astype(F32).reshape(CH, ROWS)
    slope = 0.5 * (1.0 + th) + 0.5 * nn * (1.0 - th * th) * (GC * (1.0 + 3.0 * GA * (nn * nn)))
    dn = bk_all * slope
    mean_dn = jnp.sum(dn * nn, axis=0, keepdims=True) * (1.0 / CH)
    du = rs * (dn - nn * mean_dn)
    gst = (cblk[x].astype(F32) + du).astype(BF)
    gs_s[...] = gst.reshape(8, HD, ROWS)
    gs_r[me] = gs_s[me]
    start_all(gs_s, gs_r, gs_ss, gs_rs)
    gs_out[...] = tr(gst).astype(BF)

    loop(0, 4, lambda xx: hx_recv(xx, oc).wait_recv())
    loop(1, 4, lambda r: hx_recv(lax.rem(x + r, 4), c).wait_recv())
    for cc in range(2):
        hv = lanes([h_r[cc, b] for b in range(4)] + [jnp.zeros((QC, 128), BF)]).astype(F32)
        for a in range(TAPS):
            shift = (2 - a) % EXT
            hw[cc, QC * a : QC * a + QC, :] = (pltpu.roll(hv, shift, 1) if shift else hv).astype(BF)
    co.wait_recv()
    own_c = cfull[c].reshape(384, EXT)
    oth_c = coth[...].reshape(384, EXT)
    for lo, hi in ((0, 512), (512, W5)):
        part = dot_nt(own_c, hw[c, lo:hi, :]) + dot_nt(oth_c, hw[oc, lo:hi, :])
        gp[:, :, lo:hi] = part.astype(BF).reshape(4, 96, hi - lo)

    def ys(r):
        yy = lax.rem(y + r, 4)
        return copy_to(gp.at[yy], yb.at[y], y_ss.at[yy], y_rs.at[y], y_dev(yy))

    def ys_recv(r):
        yy = lax.rem(y + r, 4)
        return copy_to(gp.at[yy], yb.at[yy], y_ss.at[yy], y_rs.at[yy], y_dev(yy))

    loop(1, 4, lambda r: ys(r).start())

    recv_all(gs_s, gs_r, gs_ss, gs_rs)
    dqa[...] = jnp.zeros_like(dqa)
    deltas = []
    for ib in range(4):
        gsb = lanes([gs_r[2 * ib], gs_r[2 * ib + 1]]).astype(F32)
        deltas.append(jnp.sum(gsb * attf[ib], axis=0, keepdims=True))
    delta = lanes(deltas)
    st[0:1, :] = deltas[0]
    for ib in range(4):
        st[ib : ib + 1, :] = deltas[ib]

    def ds_ex(t, p):
        return copy_to(d_s.at[t, p], d_r.at[t, me], d_ss.at[t, p], d_rs.at[t, me], seq_dev(p))

    def out_block(t, p):
        @pl.when(p != me)
        def _():
            ds_ex(t, p).start()

        @pl.when(p == me)
        def _():
            d_r[t, me] = d_s[t, me]

    def backward(jb):
        rows = pl.ds(pl.multiple_of(256 * jb, 256), 256)
        vb = vn[rows, :]
        kb = lanes([qkv_r[0, 2 * jb], qkv_r[0, 2 * jb + 1]])
        dk = jnp.zeros((HD, 256), F32)
        dv = jnp.zeros((HD, 256), F32)
        for ib in range(4):
            gsb = lanes([gs_r[2 * ib], gs_r[2 * ib + 1]])
            dp = dot(vb, gsb)
            p = ex[ib, rows, :] * itot[ib]
            ds = (p * (dp - st[ib : ib + 1, :])).astype(BF)
            dv = dv + dot_nt(gsb, p.astype(BF))
            dk = dk + dot_nt(pair(qkv_r, 1, ib), ds)
            dqa[:, 256 * ib : 256 * ib + 256] += dot(kb, ds)
        dkb = (dk * SCALE).astype(BF)
        dvb = dv.astype(BF)
        for half in range(2):
            p = 2 * jb + half
            d_s[0, p] = dkb[:, 128 * half : 128 * half + 128]
            d_s[1, p] = dvb[:, 128 * half : 128 * half + 128]
            out_block(0, p)
            out_block(1, p)

    loop(0, 2, backward)

    loop(1, 4, lambda r: ys_recv(r).wait_recv())
    acc = gp[y].astype(F32)
    for r in range(1, 4):
        acc = acc + yb[lax.rem(y + r, 4)].astype(F32)
    zs[...] = acc.astype(BF).reshape(2, 48, W5)
    owner = lax.div(zl, 2) == c

    def zsend(kk):
        r = lax.rem(zl - (2 * c + kk) + 4, 4)
        step = 4 * lax.div(r, 3) - r
        return r, copy_to(zs.at[kk], zb.at[r], z_ss.at[kk], z_rs.at[r], z_dev(step))

    for kk in range(2):
        r, cp = zsend(kk)

        @pl.when(r != 0)
        def _():
            cp.start()

    loop(2, 4, backward)

    dq_all = (dqa[...] * SCALE).astype(BF)
    for p in range(8):
        d_s[2, p] = dq_all[:, 128 * p : 128 * p + 128]
        out_block(2, p)

    def mx():
        return copy_to(ms, mb, m_ss, m_rs, seq_dev(lax.rem(me + 4, 8)))

    def fx(xx, cc):
        return copy_to(fs.at[cc], ob.at[x], f_ss.at[cc, xx], f_rs.at[x], xc_dev(xx, cc))

    def fx_recv(xx):
        return copy_to(fs.at[c], ob.at[xx], f_ss.at[c, xx], f_rs.at[xx], xc_dev(xx, c))

    @pl.when(owner)
    def _():
        for r, step in ((1, 1), (2, 2), (3, -1)):
            copy_to(zs.at[0], zb.at[r], z_ss.at[0], z_rs.at[r], z_dev(step)).wait_recv()
        tot = zs[lax.rem(zl, 2)].astype(F32)
        for r in range(1, 4):
            tot = tot + zb[r].astype(F32)
        ms[...] = tot
        mx().start()
        mx().wait_recv()
        norm = 1.0 / jnp.sqrt(F32(32 * 1024))
        both = (ms[...] + mb[...]) * norm
        fs[...] = both.reshape(2, 24, W5)
        loop(0, 4, lambda xx: fx(xx, oc).start())
        loop(1, 4, lambda r: fx(lax.rem(x + r, 4), c).start())
        ob[x] = fs[c]

    def d_all(t):
        return d_s.at[t], d_r.at[t], d_ss.at[t], d_rs.at[t]

    for t, out in ((0, dk_out), (1, dv_out), (2, dq_out)):
        recv_all(*d_all(t))
        out[...] = tr(d_r[t].reshape(CH, ROWS)).astype(BF)

    loop(1, 4, lambda r: fx_recv(lax.rem(x + r, 4)).wait_recv())

    @pl.when(jnp.logical_not(owner))
    def _():
        fx_recv(x).wait_recv()

    for a in range(TAPS):
        gw_out[:, a, :] = lanes([ob[b, :, QC * a : QC * a + QC] for b in range(4)])

    for t in range(3):
        sent_all(*qkv(t))
        sent_all(*d_all(t))
    sent_all(att_s, att_r, att_ss, att_rs)
    sent_all(gs_s, gs_r, gs_ss, gs_rs)
    loop(1, 4, lambda r: wy(lax.rem(y + r, 4), y).wait_send())
    loop(1, 4, lambda r: cx(lax.rem(x + r, 4), x).wait_send())

    @pl.when(first)
    def _():
        loop(0, 4, lambda p: edge(p, 0).wait_send())

    @pl.when(last)
    def _():
        loop(4, 8, lambda p: edge(p, 112).wait_send())

    wz(0, 1, zl).wait_send()
    wz(1, -1, zl).wait_send()
    wz(2, far, zl).wait_send()
    wc(c).wait_send()
    co.wait_send()
    loop(1, 4, lambda r: bk(lax.rem(x + r, 4), lax.rem(x + r, 4), x).wait_send())
    loop(0, 4, lambda xx: hx(xx, oc).wait_send())
    loop(1, 4, lambda r: hx(lax.rem(x + r, 4), c).wait_send())
    loop(1, 4, lambda r: ys(r).wait_send())
    for kk in range(2):
        r, cp = zsend(kk)

        @pl.when(r != 0)
        def _():
            cp.wait_send()

    @pl.when(owner)
    def _():
        mx().wait_send()
        loop(0, 4, lambda xx: fx(xx, oc).wait_send())
        loop(1, 4, lambda r: fx(lax.rem(x + r, 4), c).wait_send())


def body(stream_in, queries, key_rows, value_rows, conv_weight, cotangent):
    x = lax.rem(lax.axis_index("seq"), 4)
    w = lax.dynamic_slice(conv_weight, (0, 0, x * QC), (24, TAPS, QC)).reshape(24, W5)
    nat = jax.ShapeDtypeStruct((ROWS, CH), BF)
    V = pltpu.VMEM
    blk = (8, HD, ROWS)
    scratch = [
        V((3,) + blk, BF), V((3,) + blk, BF),
        V((1024, HD), BF), V((1024, HD), BF),
        V((1024, 256), F32), V((4, 1024, 256), F32), V((4, 1, 256), F32), V((4, HD, 256), F32),
        V(blk, BF), V(blk, BF),
        V((4, CH, ROWS), BF), V((ROWS, CH), BF), V((2, 4, 96, EXT), BF), V((4, 96, EXT), BF),
        V((2, 4, 4, 24, W5), BF), V((W5, CH), BF),
        V((4, QC, ROWS), BF), V((4, QC, ROWS), BF),
        V((4, QC, ROWS), BF), V((2, 4, QC, ROWS), BF), V((2, W5, EXT), BF),
        V(blk, BF), V(blk, BF), V((HD, 1024), F32), V((3,) + blk, BF), V((3,) + blk, BF),
        V((4, 96, W5), BF), V((4, 96, W5), BF), V((2, 48, W5), BF), V((4, 48, W5), BF),
        V((48, W5), F32), V((48, W5), F32), V((2, 24, W5), F32), V((4, 24, W5), F32),
        V((8, 128), F32),
    ]
    D = pltpu.SemaphoreType.DMA
    sems = [
        D((3, 8)), D((3, 8)), D((8,)), D((8,)), D((8,)), D((8,)), D((3, 8)), D((3, 8)),
        D((4,)), D((4,)), D((4,)), D, D, D,
        D((4,)), D((4,)), D((3,)), D((3,)), D, D,
        D((4,)), D((4,)), D((2, 4)), D((2, 4)), D((4,)), D((4,)), D((2,)), D((4,)), D, D,
        D((2, 4)), D((4,)),
    ]
    vm = pl.BlockSpec(memory_space=pltpu.VMEM)
    gs, dq, dk, dv, gw = pl.pallas_call(
        kernel,
        out_shape=(nat, nat, nat, nat, jax.ShapeDtypeStruct((24, TAPS, CH), F32)),
        in_specs=[vm] * 6,
        out_specs=(vm,) * 5,
        scratch_shapes=scratch + sems,
        compiler_params=pltpu.CompilerParams(
            collective_id=0, has_side_effects=True, vmem_limit_bytes=48 * 1024 * 1024
        ),
    )(stream_in[0], queries[0], key_rows[0], value_rows[0], w, cotangent[0])
    return gs[None], dq[None], dk[None], dv[None], gw


def solution(mesh):
    act = P("dp", "seq", None)
    wsp = P("dp", None, None)
    return jax.shard_map(
        body,
        mesh=mesh,
        in_specs=(act, act, act, act, wsp, act),
        out_specs=(act, act, act, act, wsp),
        check_vma=False,
    )
```

```python
import jax
import jax.numpy as jnp
from jax import lax
from jax.experimental import pallas as pl
from jax.experimental.pallas import tpu as pltpu
from jax.sharding import PartitionSpec as P

HEADS = 8
HD = 96
TAPS = 5
ROWS = 128
CH = 768
QC = 192
W5 = TAPS * QC
EXT = 640
MESH = pl.DeviceIdType.MESH
F32 = jnp.float32
BF = jnp.bfloat16
NT = (((1,), (1,)), ((), ()))
SCALE = HD ** (-0.5)
LOG2E = 1.4426950408889634
GC = 0.7978845608028654
GA = 0.044715


def dot(a, b):
    return jnp.dot(a, b, preferred_element_type=F32)


def dot_nt(a, b):
    return lax.dot_general(a, b, NT, preferred_element_type=F32)


def lanes(parts):
    return jnp.concatenate(parts, axis=1)


def tr(value):
    return value.astype(F32).T


def copy_to(src, dst, send, recv, dev):
    return pltpu.make_async_remote_copy(
        src_ref=src, dst_ref=dst, send_sem=send, recv_sem=recv, device_id=dev, device_id_type=MESH
    )


def kernel(
    x_in, q_in, k_in, v_in, w_in, c_in,
    gs_hbm, dq_hbm, dk_hbm, dv_hbm, gw_hbm,
    gs_out, dq_out, dk_out, dv_out, gw_out,
    x_ref, q_ref, k_ref, v_ref, c_ref, w_ref,
    qkv_s, qkv_r, kn, vn, st, ex, itot, attf, att_s, att_r,
    cblk, hal, cfull, coth, wbuf, wt, bk_s, bk_r, h_s, h_r, hw,
    gs_s, gs_r, dqa, d_s, d_r, gp, yb, zs, zb, ms, mb, fs, ob,
    in_sem, out_sem, qkv_ss, qkv_rs, att_ss, att_rs, gs_ss, gs_rs, d_ss, d_rs,
    c_ss, c_rs, hal_ss, hal_rs, co_ss, co_rs,
    wy_ss, wy_rs, wz_ss, wz_rs, wc_ss, wc_rs,
    bk_ss, bk_rs, h_ss, h_rs, y_ss, y_rs, z_ss, z_rs, m_ss, m_rs, f_ss, f_rs,
):
    me = lax.axis_index("seq")
    dd = lax.axis_index("dp")
    zh = lax.div(me, 4)
    x = lax.rem(me, 4)
    y = lax.div(dd, 8)
    zl = lax.rem(lax.div(dd, 2), 4)
    c = lax.rem(dd, 2)
    oc = 1 - c
    z = zh * 4 + zl
    odp = y * 8 + zl * 2 + oc

    def seq_dev(p):
        return {"seq": p, "dp": dd}

    def xc_dev(xx, cc):
        return {"seq": zh * 4 + xx, "dp": y * 8 + zl * 2 + cc}

    def y_dev(yy):
        return {"seq": me, "dp": yy * 8 + zl * 2 + c}

    def z_dev(step):
        zz = lax.rem(z + step + 8, 8)
        return {"seq": lax.div(zz, 4) * 4 + x, "dp": y * 8 + lax.rem(zz, 4) * 2 + c}

    def loop(lo, hi, fn):
        def step(i, carry):
            fn(i)
            return carry

        lax.fori_loop(lo, hi, step, 0)

    todo = {}

    def owe(name, fn):
        todo[name] = fn

    def paid(name):
        todo.pop(name)()

    def finish():
        for fn in list(todo.values()):
            fn()

    def store(i, src, dst):
        save = pltpu.make_async_copy(src, dst, out_sem.at[i])
        save.start()
        owe(f"out{i}", save.wait)

    hal[...] = jnp.zeros_like(hal)
    barrier = pltpu.get_barrier_semaphore()

    def hello(dev):
        pl.semaphore_signal(barrier, inc=1, device_id=dev, device_id_type=MESH)

    loop(1, 8, lambda r: hello(seq_dev(lax.rem(me + r, 8))))
    loop(0, 4, lambda xx: hello(xc_dev(xx, oc)))
    loop(1, 4, lambda r: hello(y_dev(lax.rem(y + r, 4))))
    for step in (1, -1, 2, -2):
        hello(z_dev(step))

    loads = []
    for i, (src, dst) in enumerate(((k_in, k_ref), (q_in, q_ref), (v_in, v_ref), (c_in, c_ref), (x_in, x_ref), (w_in, w_ref))):
        load = pltpu.make_async_copy(src, dst, in_sem.at[i])
        load.start()
        loads.append(load)
    owe("x_in", loads[4].wait)
    for i, ref in enumerate((k_ref, q_ref, v_ref)):
        loads[i].wait()
        qkv_s[i] = tr(ref[...]).astype(BF).reshape(8, HD, ROWS)
    loads[5].wait()
    for xs in range(4):

        @pl.when(x == xs)
        def _():
            wbuf[c, y, zl] = lanes([w_ref[a, :, QC * xs : QC * xs + QC] for a in range(TAPS)])

    pl.semaphore_wait(barrier, 18)

    def exch(src, dst, ssem, rsem, p):
        return copy_to(src.at[p], dst.at[me], ssem.at[p], rsem.at[me], seq_dev(p))

    def exch_recv(src, dst, ssem, rsem, p):
        return copy_to(src.at[p], dst.at[p], ssem.at[p], rsem.at[p], seq_dev(p))

    def start_all(src, dst, ssem, rsem):
        loop(1, 8, lambda r: exch(src, dst, ssem, rsem, lax.rem(me + r, 8)).start())

    def recv_all(src, dst, ssem, rsem):
        loop(1, 8, lambda r: exch_recv(src, dst, ssem, rsem, lax.rem(me + r, 8)).wait_recv())

    def sent_all(src, dst, ssem, rsem):
        loop(1, 8, lambda r: exch_recv(src, dst, ssem, rsem, lax.rem(me + r, 8)).wait_send())

    def qkv(t):
        return qkv_s.at[t], qkv_r.at[t], qkv_ss.at[t], qkv_rs.at[t]

    far = 2 - 4 * c

    def wz(i, step, slot):
        return copy_to(wbuf.at[c, y, slot], wbuf.at[c, y, slot], wz_ss.at[i], wz_rs.at[i], z_dev(step))

    def wz_recv(i, step):
        wz(i, step, lax.rem(zl + step + 4, 4)).wait_recv()

    def wz_recv_all():
        wz_recv(0, -1)
        wz_recv(1, 1)
        wz_recv(2, -far)

    def wz_sent_all():
        wz(0, 1, zl).wait_send()
        wz(1, -1, zl).wait_send()
        wz(2, far, zl).wait_send()

    wz(0, 1, zl).start()
    wz(1, -1, zl).start()
    wz(2, far, zl).start()
    owe("wz_r", wz_recv_all)
    owe("wz_s", wz_sent_all)
    for t in range(3):
        start_all(*qkv(t))
        owe(f"qkv_r{t}", lambda t=t: recv_all(*qkv(t)))
        owe(f"qkv_s{t}", lambda t=t: sent_all(*qkv(t)))

    loads[3].wait()
    cblk[x] = tr(c_ref[...]).astype(BF)
    for t in range(3):
        qkv_r[t, me] = qkv_s[t, me]
    def cx(xx, slot):
        return copy_to(cblk.at[slot], cblk.at[slot], c_ss.at[xx], c_rs.at[slot], xc_dev(xx, c))

    loop(1, 4, lambda r: cx(lax.rem(x + r, 4), x).start())
    owe("cx_r", lambda: loop(1, 4, lambda r: cx(lax.rem(x + r, 4), lax.rem(x + r, 4)).wait_recv()))
    owe("cx_s", lambda: loop(1, 4, lambda r: cx(lax.rem(x + r, 4), x).wait_send()))

    def edge(p, lo):
        rows = pl.ds(lo, 16)

        return copy_to(c_ref.at[rows], hal.at[pl.ds(lo, 16)], hal_ss.at[lax.rem(p, 4)], hal_rs, seq_dev(p))

    first = jnp.logical_and(zh == 1, x == 0)
    last = jnp.logical_and(zh == 0, x == 3)

    @pl.when(first)
    def _():
        loop(0, 4, lambda p: edge(p, 0).start())

    @pl.when(last)
    def _():
        loop(4, 8, lambda p: edge(p, 112).start())

    def edge_recv():
        @pl.when(zh == 0)
        def _():
            edge(0, 0).wait_recv()

        @pl.when(zh == 1)
        def _():
            edge(0, 112).wait_recv()

    def edge_sent():
        @pl.when(first)
        def _():
            loop(0, 4, lambda p: edge(p, 0).wait_send())

        @pl.when(last)
        def _():
            loop(4, 8, lambda p: edge(p, 112).wait_send())

    owe("edge_r", edge_recv)
    owe("edge_s", edge_sent)
    paid("wz_r")

    def wy(yy, slot):
        return copy_to(wbuf.at[c, slot], wbuf.at[c, slot], wy_ss.at[yy], wy_rs.at[slot], y_dev(yy))

    loop(1, 4, lambda r: wy(lax.rem(y + r, 4), y).start())
    owe("wy_r", lambda: loop(1, 4, lambda r: wy(lax.rem(y + r, 4), lax.rem(y + r, 4)).wait_recv()))
    owe("wy_s", lambda: loop(1, 4, lambda r: wy(lax.rem(y + r, 4), y).wait_send()))

    paid("qkv_r0")
    for b in range(8):
        kn[128 * b : 128 * b + 128, :] = tr(qkv_r[0, b]).astype(BF)
    paid("qkv_r1")

    paid("qkv_r2")
    for b in range(8):
        vn[128 * b : 128 * b + 128, :] = tr(qkv_r[2, b]).astype(BF)

    def pair(ref, t, i):
        return lanes([ref[t, 2 * i], ref[t, 2 * i + 1]])

    def forward(ib):
        qb = lanes([qkv_r[1, 2 * ib], qkv_r[1, 2 * ib + 1]])
        top = None
        for jb in range(4):
            s = dot(kn[256 * jb : 256 * jb + 256, :], qb)
            st[256 * jb : 256 * jb + 256, :] = s
            m = jnp.max(s, axis=0, keepdims=True)
            top = m if top is None else jnp.maximum(top, m)
        tot = jnp.zeros((1, 256), F32)
        acc = jnp.zeros((HD, 256), F32)
        for jb in range(4):
            e = jnp.exp2((st[256 * jb : 256 * jb + 256, :] - top) * (SCALE * LOG2E))
            ex[ib, 256 * jb : 256 * jb + 256, :] = e
            tot = tot + jnp.sum(e, axis=0, keepdims=True)
            acc = acc + dot(pair(qkv_r, 2, jb), e.astype(BF))
        inv = 1.0 / tot
        itot[ib] = inv
        att = acc * inv
        attf[ib] = att
        ab = att.astype(BF)
        for half in range(2):
            p = 2 * ib + half
            att_s[p] = ab[:, 128 * half : 128 * half + 128]

            @pl.when(p != me)
            def _():
                exch(att_s, att_r, att_ss, att_rs, p).start()

            @pl.when(p == me)
            def _():
                att_r[me] = att_s[me]

    loop(0, 4, forward)
    owe("att_r", lambda: recv_all(att_s, att_r, att_ss, att_rs))
    owe("att_s", lambda: sent_all(att_s, att_r, att_ss, att_rs))

    paid("wy_r")

    def wc(slot):
        return copy_to(wbuf.at[slot], wbuf.at[slot], wc_ss, wc_rs, xc_dev(x, oc))

    wc(c).start()
    owe("wc_r", lambda: wc(oc).wait_recv())
    owe("wc_s", lambda: wc(c).wait_send())

    paid("cx_r")
    paid("edge_r")
    halt = tr(hal[...]).astype(BF)
    for cc in range(2):
        for yy in range(4):
            lo = 192 * yy + 96 * cc
            for b in range(4):
                cfull[cc, yy, :, 128 * b : 128 * b + 128] = cblk[b, lo : lo + 96, :]
            cfull[cc, yy, :, 512:640] = halt[lo : lo + 96, :]

    co = copy_to(cfull.at[oc], coth, co_ss, co_rs, xc_dev(x, oc))
    co.start()
    owe("co_r", co.wait_recv)
    owe("co_s", co.wait_send)

    paid("wc_r")
    for n in range(8):
        width = min(128, W5 - 128 * n)
        rows = []
        for cc in range(2):
            for yy in range(4):
                for j in range(4):
                    rows.append(wbuf[j % 2, yy, 2 * cc + j // 2, :, 128 * n : 128 * n + width].astype(F32))
        wt[128 * n : 128 * n + width, :] = jnp.concatenate(rows, axis=0).T.astype(BF)

    cot_all = cfull[...].reshape(CH, EXT)
    back_q = None
    for a in range(TAPS):
        part = dot(wt[QC * a : QC * a + QC, :], cot_all)
        shift = (a - 2) % EXT
        if shift:
            part = pltpu.roll(part, shift, 1)
        back_q = part if back_q is None else back_q + part
    back_b = back_q.astype(BF)
    for b in range(4):
        bk_s[b] = back_b[:, 128 * b : 128 * b + 128]
    bk_r[x] = bk_s[x]

    def bk(xx, slot_from, slot_to):
        return copy_to(bk_s.at[slot_from], bk_r.at[slot_to], bk_ss.at[xx], bk_rs.at[slot_to], xc_dev(xx, c))

    def bk_start(r):
        xx = lax.rem(x + r, 4)
        bk(xx, xx, x).start()

    def bk_wait(r):
        xx = lax.rem(x + r, 4)
        bk(xx, xx, xx).wait_recv()

    loop(1, 4, bk_start)
    owe("bk_r", lambda: loop(1, 4, bk_wait))
    owe("bk_s", lambda: loop(1, 4, lambda r: bk(lax.rem(x + r, 4), lax.rem(x + r, 4), x).wait_send()))

    paid("x_in")
    xt = tr(x_ref[...])
    paid("att_r")
    u = (xt + att_r[...].astype(F32).reshape(CH, ROWS)).astype(BF).astype(F32)
    rs = lax.rsqrt(jnp.mean(u * u, axis=0, keepdims=True) + 1e-6)
    nn = u * rs
    th = jnp.tanh(GC * (nn + GA * (nn * nn * nn)))
    hid = (0.5 * nn * (1.0 + th)).astype(BF)
    h_s[...] = hid.reshape(4, QC, ROWS)
    h_r[c, x] = h_s[x]

    def hx(xx, cc):
        return copy_to(h_s.at[xx], h_r.at[c, x], h_ss.at[cc, xx], h_rs.at[c, x], xc_dev(xx, cc))

    def hx_recv(xx, cc):
        return copy_to(h_s.at[xx], h_r.at[cc, xx], h_ss.at[cc, xx], h_rs.at[cc, xx], xc_dev(xx, cc))

    loop(0, 4, lambda xx: hx(xx, oc).start())
    loop(1, 4, lambda r: hx(lax.rem(x + r, 4), c).start())

    def hx_recv_all():
        loop(0, 4, lambda xx: hx_recv(xx, oc).wait_recv())
        loop(1, 4, lambda r: hx_recv(lax.rem(x + r, 4), c).wait_recv())

    def hx_sent_all():
        loop(0, 4, lambda xx: hx(xx, oc).wait_send())
        loop(1, 4, lambda r: hx(lax.rem(x + r, 4), c).wait_send())

    owe("hx_r", hx_recv_all)
    owe("hx_s", hx_sent_all)

    paid("bk_r")
    bk_all = bk_r[...].astype(F32).reshape(CH, ROWS)
    slope = 0.5 * (1.0 + th) + 0.5 * nn * (1.0 - th * th) * (GC * (1.0 + 3.0 * GA * (nn * nn)))
    dn = bk_all * slope
    mean_dn = jnp.sum(dn * nn, axis=0, keepdims=True) * (1.0 / CH)
    du = rs * (dn - nn * mean_dn)
    gst = (cblk[x].astype(F32) + du).astype(BF)
    gs_s[...] = gst.reshape(8, HD, ROWS)
    gs_r[me] = gs_s[me]
    start_all(gs_s, gs_r, gs_ss, gs_rs)
    owe("gs_r", lambda: recv_all(gs_s, gs_r, gs_ss, gs_rs))
    owe("gs_s", lambda: sent_all(gs_s, gs_r, gs_ss, gs_rs))

    gs_out[...] = tr(gst).astype(BF)
    store(0, gs_out, gs_hbm)

    paid("hx_r")
    for cc in range(2):
        hv = lanes([h_r[cc, b] for b in range(4)] + [jnp.zeros((QC, 128), BF)]).astype(F32)
        for a in range(TAPS):
            shift = (2 - a) % EXT
            hw[cc, QC * a : QC * a + QC, :] = (pltpu.roll(hv, shift, 1) if shift else hv).astype(BF)
    paid("co_r")
    own_c = cfull[c].reshape(384, EXT)
    oth_c = coth[...].reshape(384, EXT)
    for lo, hi in ((0, 512), (512, W5)):
        part = dot_nt(own_c, hw[c, lo:hi, :]) + dot_nt(oth_c, hw[oc, lo:hi, :])
        gp[:, :, lo:hi] = part.astype(BF).reshape(4, 96, hi - lo)

    def ys(r):
        yy = lax.rem(y + r, 4)
        return copy_to(gp.at[yy], yb.at[y], y_ss.at[yy], y_rs.at[y], y_dev(yy))

    def ys_recv(r):
        yy = lax.rem(y + r, 4)
        return copy_to(gp.at[yy], yb.at[yy], y_ss.at[yy], y_rs.at[yy], y_dev(yy))

    loop(1, 4, lambda r: ys(r).start())
    owe("ys_r", lambda: loop(1, 4, lambda r: ys_recv(r).wait_recv()))
    owe("ys_s", lambda: loop(1, 4, lambda r: ys(r).wait_send()))

    paid("gs_r")
    dqa[...] = jnp.zeros_like(dqa)
    deltas = []
    for ib in range(4):
        gsb = lanes([gs_r[2 * ib], gs_r[2 * ib + 1]]).astype(F32)
        deltas.append(jnp.sum(gsb * attf[ib], axis=0, keepdims=True))
    delta = lanes(deltas)
    st[0:1, :] = deltas[0]
    for ib in range(4):
        st[ib : ib + 1, :] = deltas[ib]

    def ds_ex(t, p):
        return copy_to(d_s.at[t, p], d_r.at[t, me], d_ss.at[t, p], d_rs.at[t, me], seq_dev(p))

    def out_block(t, p):
        @pl.when(p != me)
        def _():
            ds_ex(t, p).start()

        @pl.when(p == me)
        def _():
            d_r[t, me] = d_s[t, me]

    def backward(jb):
        rows = pl.ds(pl.multiple_of(256 * jb, 256), 256)
        vb = vn[rows, :]
        kb = lanes([qkv_r[0, 2 * jb], qkv_r[0, 2 * jb + 1]])
        dk = jnp.zeros((HD, 256), F32)
        dv = jnp.zeros((HD, 256), F32)
        for ib in range(4):
            gsb = lanes([gs_r[2 * ib], gs_r[2 * ib + 1]])
            dp = dot(vb, gsb)
            p = ex[ib, rows, :] * itot[ib]
            ds = (p * (dp - st[ib : ib + 1, :])).astype(BF)
            dv = dv + dot_nt(gsb, p.astype(BF))
            dk = dk + dot_nt(pair(qkv_r, 1, ib), ds)
            dqa[:, 256 * ib : 256 * ib + 256] += dot(kb, ds)
        dkb = (dk * SCALE).astype(BF)
        dvb = dv.astype(BF)
        for half in range(2):
            p = 2 * jb + half
            d_s[0, p] = dkb[:, 128 * half : 128 * half + 128]
            d_s[1, p] = dvb[:, 128 * half : 128 * half + 128]
            out_block(0, p)
            out_block(1, p)

    loop(0, 4, backward)
    dq_all = (dqa[...] * SCALE).astype(BF)
    for p in range(8):
        d_s[2, p] = dq_all[:, 128 * p : 128 * p + 128]
        out_block(2, p)

    def d_all(t):
        return d_s.at[t], d_r.at[t], d_ss.at[t], d_rs.at[t]

    for t in range(3):
        owe(f"d_r{t}", lambda t=t: recv_all(*d_all(t)))
        owe(f"d_s{t}", lambda t=t: sent_all(*d_all(t)))

    paid("ys_r")
    acc = gp[y].astype(F32)
    for r in range(1, 4):
        acc = acc + yb[lax.rem(y + r, 4)].astype(F32)
    zs[...] = acc.astype(BF).reshape(2, 48, W5)
    owner = lax.div(zl, 2) == c

    def zsend(kk):
        r = lax.rem(zl - (2 * c + kk) + 4, 4)
        step = 4 * lax.div(r, 3) - r
        return r, copy_to(zs.at[kk], zb.at[r], z_ss.at[kk], z_rs.at[r], z_dev(step))

    for kk in range(2):
        r, cp = zsend(kk)

        @pl.when(r != 0)
        def _():
            cp.start()

    def zs_sent():
        for kk in range(2):
            r, cp = zsend(kk)

            @pl.when(r != 0)
            def _():
                cp.wait_send()

    owe("zs_s", zs_sent)

    def mx():
        return copy_to(ms, mb, m_ss, m_rs, seq_dev(lax.rem(me + 4, 8)))

    def fx(xx, cc):
        return copy_to(fs.at[cc], ob.at[x], f_ss.at[cc, xx], f_rs.at[x], xc_dev(xx, cc))

    def fx_recv(xx):
        return copy_to(fs.at[c], ob.at[xx], f_ss.at[c, xx], f_rs.at[xx], xc_dev(xx, c))

    def zs_recv():
        for r, step in ((1, 1), (2, 2), (3, -1)):
            copy_to(zs.at[0], zb.at[r], z_ss.at[0], z_rs.at[r], z_dev(step)).wait_recv()

    @pl.when(owner)
    def _():
        for r, step in ((1, 1), (2, 2), (3, -1)):
            copy_to(zs.at[0], zb.at[r], z_ss.at[0], z_rs.at[r], z_dev(step)).wait_recv()
        tot = zs[lax.rem(zl, 2)].astype(F32)
        for r in range(1, 4):
            tot = tot + zb[r].astype(F32)
        ms[...] = tot.astype(BF)
        mx().start()
        mx().wait_recv()
        norm = 1.0 / jnp.sqrt(F32(32 * 1024))
        both = (ms[...].astype(F32) + mb[...].astype(F32)) * norm
        fs[...] = both.reshape(2, 24, W5).astype(BF)
        loop(0, 4, lambda xx: fx(xx, oc).start())
        loop(1, 4, lambda r: fx(lax.rem(x + r, 4), c).start())
        ob[x] = fs[c]

    def own_sent():
        @pl.when(owner)
        def _():
            mx().wait_send()
            loop(0, 4, lambda xx: fx(xx, oc).wait_send())
            loop(1, 4, lambda r: fx(lax.rem(x + r, 4), c).wait_send())

    owe("own_s", own_sent)

    for t, out, there in ((0, dk_out, dk_hbm), (1, dv_out, dv_hbm), (2, dq_out, dq_hbm)):
        paid(f"d_r{t}")
        out[...] = tr(d_r[t].reshape(CH, ROWS)).astype(BF)
        store(1 + t, out, there)

    loop(1, 4, lambda r: fx_recv(lax.rem(x + r, 4)).wait_recv())

    @pl.when(jnp.logical_not(owner))
    def _():
        fx_recv(x).wait_recv()

    for a in range(TAPS):
        gw_out[a] = lanes([ob[b, :, QC * a : QC * a + QC].astype(F32) for b in range(4)])

    store(4, gw_out, gw_hbm)

    finish()


def hand_over(*refs):
    ins, outs, held, sem = refs[:5], refs[5:10], refs[10:15], refs[15]
    reads = [pltpu.make_async_copy(ins[i], held[i], sem.at[0, i]) for i in range(5)]
    writes = [pltpu.make_async_copy(held[i], outs[i], sem.at[1, i]) for i in range(5)]
    for read in reads:
        read.start()
    for read, write in zip(reads, writes):
        read.wait()
        write.start()
    for write in writes:
        write.wait()


def body(stream_in, queries, key_rows, value_rows, conv_weight, cotangent):
    nat = jax.ShapeDtypeStruct((ROWS, CH), BF)
    V = pltpu.VMEM
    blk = (8, HD, ROWS)
    scratch = [V((ROWS, CH), BF) for _ in range(4)] + [
        V((TAPS, 24, CH), F32),
    ] + [V((ROWS, CH), BF) for _ in range(5)] + [
        V((TAPS, 24, CH), BF),
        V((3,) + blk, BF), V((3,) + blk, BF),
        V((1024, HD), BF), V((1024, HD), BF),
        V((1024, 256), F32), V((4, 1024, 256), F32), V((4, 1, 256), F32), V((4, HD, 256), F32),
        V(blk, BF), V(blk, BF),
        V((4, CH, ROWS), BF), V((ROWS, CH), BF), V((2, 4, 96, EXT), BF), V((4, 96, EXT), BF),
        V((2, 4, 4, 24, W5), BF), V((W5, CH), BF),
        V((4, QC, ROWS), BF), V((4, QC, ROWS), BF),
        V((4, QC, ROWS), BF), V((2, 4, QC, ROWS), BF), V((2, W5, EXT), BF),
        V(blk, BF), V(blk, BF), V((HD, 1024), F32), V((3,) + blk, BF), V((3,) + blk, BF),
        V((4, 96, W5), BF), V((4, 96, W5), BF), V((2, 48, W5), BF), V((4, 48, W5), BF),
        V((48, W5), BF), V((48, W5), BF), V((2, 24, W5), BF), V((4, 24, W5), BF),
    ]
    D = pltpu.SemaphoreType.DMA
    sems = [
        D((6,)), D((5,)), D((3, 8)), D((3, 8)), D((8,)), D((8,)), D((8,)), D((8,)), D((3, 8)), D((3, 8)),
        D((4,)), D((4,)), D((4,)), D, D, D,
        D((4,)), D((4,)), D((3,)), D((3,)), D, D,
        D((4,)), D((4,)), D((2, 4)), D((2, 4)), D((4,)), D((4,)), D((2,)), D((4,)), D, D,
        D((2, 4)), D((4,)),
    ]
    hbm = pl.BlockSpec(memory_space=pl.ANY)
    shapes = (nat, nat, nat, nat, jax.ShapeDtypeStruct((TAPS, 24, CH), F32))
    made = pl.pallas_call(
        kernel,
        out_shape=shapes,
        in_specs=[hbm] * 6,
        out_specs=(hbm,) * 5,
        scratch_shapes=scratch + sems,
        compiler_params=pltpu.CompilerParams(
            collective_id=0, has_side_effects=True, vmem_limit_bytes=58 * 1024 * 1024
        ),
    )(stream_in[0], queries[0], key_rows[0], value_rows[0], jnp.transpose(conv_weight, (1, 0, 2)), cotangent[0])
    gs, dq, dk, dv, gw = pl.pallas_call(
        hand_over,
        out_shape=shapes,
        in_specs=[hbm] * 5,
        out_specs=(hbm,) * 5,
        scratch_shapes=[V((ROWS, CH), BF) for _ in range(4)] + [V((TAPS, 24, CH), F32), D((2, 5))],
    )(*made)
    return gs[None], dq[None], dk[None], dv[None], jnp.transpose(gw, (1, 0, 2))


def solution(mesh):
    act = P("dp", "seq", None)
    wsp = P("dp", None, None)
    return jax.shard_map(
        body,
        mesh=mesh,
        in_specs=(act, act, act, act, wsp, act),
        out_specs=(act, act, act, act, wsp),
        check_vma=False,
    )
```

```python
import jax
import jax.numpy as jnp
from jax import lax
from jax.experimental import pallas as pl
from jax.experimental.pallas import tpu as pltpu
from jax.sharding import PartitionSpec as P

HEADS = 8
HD = 96
TAPS = 5
ROWS = 128
CH = 768
QC = 192
W5 = TAPS * QC
EXT = 640
MESH = pl.DeviceIdType.MESH
F32 = jnp.float32
BF = jnp.bfloat16
NT = (((1,), (1,)), ((), ()))
SCALE = HD ** (-0.5)
LOG2E = 1.4426950408889634
GC = 0.7978845608028654
GA = 0.044715


def dot(a, b):
    return jnp.dot(a, b, preferred_element_type=F32)


def dot_nt(a, b):
    return lax.dot_general(a, b, NT, preferred_element_type=F32)


def lanes(parts):
    return jnp.concatenate(parts, axis=1)


def tr(value):
    return value.astype(F32).T


def copy_to(src, dst, send, recv, dev):
    return pltpu.make_async_remote_copy(
        src_ref=src, dst_ref=dst, send_sem=send, recv_sem=recv, device_id=dev, device_id_type=MESH
    )


def kernel(
    x_in, q_in, k_in, v_in, w_in, c_in,
    gs_hbm, dq_hbm, dk_hbm, dv_hbm, gw_hbm,
    gs_out, dq_out, dk_out, dv_out, gw_out,
    x_ref, q_ref, k_ref, v_ref, c_ref, w_ref,
    qkv_s, qkv_r, kn, vn, st, ex, itot, attf, att_s, att_r,
    cblk, hal, cfull, coth, wbuf, wt, bk_s, bk_r, h_s, h_r, hw,
    gs_s, gs_r, dqa, d_s, d_r, gp, yb, zs, zb, ms, mb, fs, ob,
    in_sem, out_sem, qkv_ss, qkv_rs, att_ss, att_rs, gs_ss, gs_rs, d_ss, d_rs,
    c_ss, c_rs, hal_ss, hal_rs, co_ss, co_rs,
    wy_ss, wy_rs, wz_ss, wz_rs, wc_ss, wc_rs,
    bk_ss, bk_rs, h_ss, h_rs, y_ss, y_rs, z_ss, z_rs, m_ss, m_rs, f_ss, f_rs,
):
    me = lax.axis_index("seq")
    dd = lax.axis_index("dp")
    zh = lax.div(me, 4)
    x = lax.rem(me, 4)
    y = lax.div(dd, 8)
    zl = lax.rem(lax.div(dd, 2), 4)
    c = lax.rem(dd, 2)
    oc = 1 - c
    z = zh * 4 + zl
    odp = y * 8 + zl * 2 + oc

    def seq_dev(p):
        return {"seq": p, "dp": dd}

    def xc_dev(xx, cc):
        return {"seq": zh * 4 + xx, "dp": y * 8 + zl * 2 + cc}

    def y_dev(yy):
        return {"seq": me, "dp": yy * 8 + zl * 2 + c}

    def z_dev(step):
        zz = lax.rem(z + step + 8, 8)
        return {"seq": lax.div(zz, 4) * 4 + x, "dp": y * 8 + lax.rem(zz, 4) * 2 + c}

    def loop(lo, hi, fn):
        def step(i, carry):
            fn(i)
            return carry

        lax.fori_loop(lo, hi, step, 0)

    todo = {}

    def owe(name, fn):
        todo[name] = fn

    def paid(name):
        todo.pop(name)()

    def finish():
        for fn in list(todo.values()):
            fn()

    def store(i, src, dst):
        save = pltpu.make_async_copy(src, dst, out_sem.at[i])
        save.start()
        owe(f"out{i}", save.wait)

    hal[...] = jnp.zeros_like(hal)
    barrier = pltpu.get_barrier_semaphore()

    def hello(dev):
        pl.semaphore_signal(barrier, inc=1, device_id=dev, device_id_type=MESH)

    loop(1, 8, lambda r: hello(seq_dev(lax.rem(me + r, 8))))
    loop(0, 4, lambda xx: hello(xc_dev(xx, oc)))
    loop(1, 4, lambda r: hello(y_dev(lax.rem(y + r, 4))))
    for step in (1, -1, 2, -2):
        hello(z_dev(step))

    loads = []
    for i, (src, dst) in enumerate(((k_in, k_ref), (q_in, q_ref), (v_in, v_ref), (c_in, c_ref), (x_in, x_ref), (w_in, w_ref))):
        load = pltpu.make_async_copy(src, dst, in_sem.at[i])
        load.start()
        loads.append(load)
    owe("x_in", loads[4].wait)
    for i, ref in enumerate((k_ref, q_ref, v_ref)):
        loads[i].wait()
        qkv_s[i] = tr(ref[...]).astype(BF).reshape(8, HD, ROWS)
    loads[5].wait()
    for xs in range(4):

        @pl.when(x == xs)
        def _():
            wbuf[c, y, zl] = lanes([w_ref[a, :, QC * xs : QC * xs + QC] for a in range(TAPS)])

    pl.semaphore_wait(barrier, 18)

    def exch(src, dst, ssem, rsem, p):
        return copy_to(src.at[p], dst.at[me], ssem.at[p], rsem.at[me], seq_dev(p))

    def exch_recv(src, dst, ssem, rsem, p):
        return copy_to(src.at[p], dst.at[p], ssem.at[p], rsem.at[p], seq_dev(p))

    def start_all(src, dst, ssem, rsem):
        loop(1, 8, lambda r: exch(src, dst, ssem, rsem, lax.rem(me + r, 8)).start())

    def recv_all(src, dst, ssem, rsem):
        loop(1, 8, lambda r: exch_recv(src, dst, ssem, rsem, lax.rem(me + r, 8)).wait_recv())

    def sent_all(src, dst, ssem, rsem):
        loop(1, 8, lambda r: exch_recv(src, dst, ssem, rsem, lax.rem(me + r, 8)).wait_send())

    def qkv(t):
        return qkv_s.at[t], qkv_r.at[t], qkv_ss.at[t], qkv_rs.at[t]

    far = 2 - 4 * c

    def wz(i, step, slot):
        return copy_to(wbuf.at[c, y, slot], wbuf.at[c, y, slot], wz_ss.at[i], wz_rs.at[i], z_dev(step))

    def wz_recv(i, step):
        wz(i, step, lax.rem(zl + step + 4, 4)).wait_recv()

    def wz_recv_all():
        wz_recv(0, -1)
        wz_recv(1, 1)
        wz_recv(2, -far)

    def wz_sent_all():
        wz(0, 1, zl).wait_send()
        wz(1, -1, zl).wait_send()
        wz(2, far, zl).wait_send()

    def start_qkv(t):
        start_all(*qkv(t))
        owe(f"qkv_r{t}", lambda: recv_all(*qkv(t)))
        owe(f"qkv_s{t}", lambda: sent_all(*qkv(t)))

    start_qkv(0)
    wz(0, 1, zl).start()
    wz(1, -1, zl).start()
    wz(2, far, zl).start()
    owe("wz_r", wz_recv_all)
    owe("wz_s", wz_sent_all)
    paid("wz_r")

    def wy(yy, slot):
        return copy_to(wbuf.at[c, slot], wbuf.at[c, slot], wy_ss.at[yy], wy_rs.at[slot], y_dev(yy))

    loop(1, 4, lambda r: wy(lax.rem(y + r, 4), y).start())
    owe("wy_r", lambda: loop(1, 4, lambda r: wy(lax.rem(y + r, 4), lax.rem(y + r, 4)).wait_recv()))
    owe("wy_s", lambda: loop(1, 4, lambda r: wy(lax.rem(y + r, 4), y).wait_send()))

    start_qkv(1)
    start_qkv(2)
    loads[3].wait()
    cblk[x] = tr(c_ref[...]).astype(BF)
    for t in range(3):
        qkv_r[t, me] = qkv_s[t, me]
    def cx(xx, slot):
        return copy_to(cblk.at[slot], cblk.at[slot], c_ss.at[xx], c_rs.at[slot], xc_dev(xx, c))

    loop(1, 4, lambda r: cx(lax.rem(x + r, 4), x).start())
    owe("cx_r", lambda: loop(1, 4, lambda r: cx(lax.rem(x + r, 4), lax.rem(x + r, 4)).wait_recv()))
    owe("cx_s", lambda: loop(1, 4, lambda r: cx(lax.rem(x + r, 4), x).wait_send()))

    def edge(p, lo):
        rows = pl.ds(lo, 16)

        return copy_to(c_ref.at[rows], hal.at[pl.ds(lo, 16)], hal_ss.at[lax.rem(p, 4)], hal_rs, seq_dev(p))

    first = jnp.logical_and(zh == 1, x == 0)
    last = jnp.logical_and(zh == 0, x == 3)

    @pl.when(first)
    def _():
        loop(0, 4, lambda p: edge(p, 0).start())

    @pl.when(last)
    def _():
        loop(4, 8, lambda p: edge(p, 112).start())

    def edge_recv():
        @pl.when(zh == 0)
        def _():
            edge(0, 0).wait_recv()

        @pl.when(zh == 1)
        def _():
            edge(0, 112).wait_recv()

    def edge_sent():
        @pl.when(first)
        def _():
            loop(0, 4, lambda p: edge(p, 0).wait_send())

        @pl.when(last)
        def _():
            loop(4, 8, lambda p: edge(p, 112).wait_send())

    owe("edge_r", edge_recv)
    owe("edge_s", edge_sent)
    paid("qkv_r0")
    for b in range(8):
        kn[128 * b : 128 * b + 128, :] = tr(qkv_r[0, b]).astype(BF)
    paid("qkv_r1")

    paid("qkv_r2")
    for b in range(8):
        vn[128 * b : 128 * b + 128, :] = tr(qkv_r[2, b]).astype(BF)

    def pair(ref, t, i):
        return lanes([ref[t, 2 * i], ref[t, 2 * i + 1]])

    def forward(ib):
        qb = lanes([qkv_r[1, 2 * ib], qkv_r[1, 2 * ib + 1]])
        top = None
        for jb in range(4):
            s = dot(kn[256 * jb : 256 * jb + 256, :], qb)
            st[256 * jb : 256 * jb + 256, :] = s
            m = jnp.max(s, axis=0, keepdims=True)
            top = m if top is None else jnp.maximum(top, m)
        tot = jnp.zeros((1, 256), F32)
        acc = jnp.zeros((HD, 256), F32)
        for jb in range(4):
            e = jnp.exp2((st[256 * jb : 256 * jb + 256, :] - top) * (SCALE * LOG2E))
            ex[ib, 256 * jb : 256 * jb + 256, :] = e
            tot = tot + jnp.sum(e, axis=0, keepdims=True)
            acc = acc + dot(pair(qkv_r, 2, jb), e.astype(BF))
        inv = 1.0 / tot
        itot[ib] = inv
        att = acc * inv
        attf[ib] = att
        ab = att.astype(BF)
        for half in range(2):
            p = 2 * ib + half
            att_s[p] = ab[:, 128 * half : 128 * half + 128]

            @pl.when(p != me)
            def _():
                exch(att_s, att_r, att_ss, att_rs, p).start()

            @pl.when(p == me)
            def _():
                att_r[me] = att_s[me]

    loop(0, 4, forward)
    owe("att_r", lambda: recv_all(att_s, att_r, att_ss, att_rs))
    owe("att_s", lambda: sent_all(att_s, att_r, att_ss, att_rs))

    paid("wy_r")

    def wc(slot):
        return copy_to(wbuf.at[slot], wbuf.at[slot], wc_ss, wc_rs, xc_dev(x, oc))

    wc(c).start()
    owe("wc_r", lambda: wc(oc).wait_recv())
    owe("wc_s", lambda: wc(c).wait_send())

    paid("cx_r")
    paid("edge_r")
    halt = tr(hal[...]).astype(BF)
    for cc in range(2):
        for yy in range(4):
            lo = 192 * yy + 96 * cc
            for b in range(4):
                cfull[cc, yy, :, 128 * b : 128 * b + 128] = cblk[b, lo : lo + 96, :]
            cfull[cc, yy, :, 512:640] = halt[lo : lo + 96, :]

    co = copy_to(cfull.at[oc], coth, co_ss, co_rs, xc_dev(x, oc))
    co.start()
    owe("co_r", co.wait_recv)
    owe("co_s", co.wait_send)

    paid("wc_r")
    for n in range(8):
        width = min(128, W5 - 128 * n)
        rows = []
        for cc in range(2):
            for yy in range(4):
                for j in range(4):
                    rows.append(wbuf[j % 2, yy, 2 * cc + j // 2, :, 128 * n : 128 * n + width].astype(F32))
        wt[128 * n : 128 * n + width, :] = jnp.concatenate(rows, axis=0).T.astype(BF)

    cot_all = cfull[...].reshape(CH, EXT)
    back_q = None
    for a in range(TAPS):
        part = dot(wt[QC * a : QC * a + QC, :], cot_all)
        shift = (a - 2) % EXT
        if shift:
            part = pltpu.roll(part, shift, 1)
        back_q = part if back_q is None else back_q + part
    back_b = back_q.astype(BF)
    for b in range(4):
        bk_s[b] = back_b[:, 128 * b : 128 * b + 128]
    bk_r[x] = bk_s[x]

    def bk(xx, slot_from, slot_to):
        return copy_to(bk_s.at[slot_from], bk_r.at[slot_to], bk_ss.at[xx], bk_rs.at[slot_to], xc_dev(xx, c))

    def bk_start(r):
        xx = lax.rem(x + r, 4)
        bk(xx, xx, x).start()

    def bk_wait(r):
        xx = lax.rem(x + r, 4)
        bk(xx, xx, xx).wait_recv()

    loop(1, 4, bk_start)
    owe("bk_r", lambda: loop(1, 4, bk_wait))
    owe("bk_s", lambda: loop(1, 4, lambda r: bk(lax.rem(x + r, 4), lax.rem(x + r, 4), x).wait_send()))

    paid("x_in")
    xt = tr(x_ref[...])
    paid("att_r")
    u = (xt + att_r[...].astype(F32).reshape(CH, ROWS)).astype(BF).astype(F32)
    rs = lax.rsqrt(jnp.mean(u * u, axis=0, keepdims=True) + 1e-6)
    nn = u * rs
    th = jnp.tanh(GC * (nn + GA * (nn * nn * nn)))
    hid = (0.5 * nn * (1.0 + th)).astype(BF)
    h_s[...] = hid.reshape(4, QC, ROWS)
    h_r[c, x] = h_s[x]

    def hx(xx, cc):
        return copy_to(h_s.at[xx], h_r.at[c, x], h_ss.at[cc, xx], h_rs.at[c, x], xc_dev(xx, cc))

    def hx_recv(xx, cc):
        return copy_to(h_s.at[xx], h_r.at[cc, xx], h_ss.at[cc, xx], h_rs.at[cc, xx], xc_dev(xx, cc))

    loop(0, 4, lambda xx: hx(xx, oc).start())
    loop(1, 4, lambda r: hx(lax.rem(x + r, 4), c).start())

    def hx_recv_all():
        loop(0, 4, lambda xx: hx_recv(xx, oc).wait_recv())
        loop(1, 4, lambda r: hx_recv(lax.rem(x + r, 4), c).wait_recv())

    def hx_sent_all():
        loop(0, 4, lambda xx: hx(xx, oc).wait_send())
        loop(1, 4, lambda r: hx(lax.rem(x + r, 4), c).wait_send())

    owe("hx_r", hx_recv_all)
    owe("hx_s", hx_sent_all)

    paid("bk_r")
    bk_all = bk_r[...].astype(F32).reshape(CH, ROWS)
    slope = 0.5 * (1.0 + th) + 0.5 * nn * (1.0 - th * th) * (GC * (1.0 + 3.0 * GA * (nn * nn)))
    dn = bk_all * slope
    mean_dn = jnp.sum(dn * nn, axis=0, keepdims=True) * (1.0 / CH)
    du = rs * (dn - nn * mean_dn)
    gst = (cblk[x].astype(F32) + du).astype(BF)
    gs_s[...] = gst.reshape(8, HD, ROWS)
    gs_r[me] = gs_s[me]
    start_all(gs_s, gs_r, gs_ss, gs_rs)
    owe("gs_r", lambda: recv_all(gs_s, gs_r, gs_ss, gs_rs))
    owe("gs_s", lambda: sent_all(gs_s, gs_r, gs_ss, gs_rs))

    gs_out[...] = tr(gst).astype(BF)
    store(0, gs_out, gs_hbm)

    paid("hx_r")
    for cc in range(2):
        hv = lanes([h_r[cc, b] for b in range(4)] + [jnp.zeros((QC, 128), BF)]).astype(F32)
        for a in range(TAPS):
            shift = (2 - a) % EXT
            hw[cc, QC * a : QC * a + QC, :] = (pltpu.roll(hv, shift, 1) if shift else hv).astype(BF)
    paid("co_r")
    own_c = cfull[c].reshape(384, EXT)
    oth_c = coth[...].reshape(384, EXT)
    for lo, hi in ((0, 512), (512, W5)):
        part = dot_nt(own_c, hw[c, lo:hi, :]) + dot_nt(oth_c, hw[oc, lo:hi, :])
        gp[:, :, lo:hi] = part.astype(BF).reshape(4, 96, hi - lo)

    def ys(r):
        yy = lax.rem(y + r, 4)
        return copy_to(gp.at[yy], yb.at[y], y_ss.at[yy], y_rs.at[y], y_dev(yy))

    def ys_recv(r):
        yy = lax.rem(y + r, 4)
        return copy_to(gp.at[yy], yb.at[yy], y_ss.at[yy], y_rs.at[yy], y_dev(yy))

    loop(1, 4, lambda r: ys(r).start())
    owe("ys_r", lambda: loop(1, 4, lambda r: ys_recv(r).wait_recv()))
    owe("ys_s", lambda: loop(1, 4, lambda r: ys(r).wait_send()))

    paid("gs_r")
    dqa[...] = jnp.zeros_like(dqa)
    deltas = []
    for ib in range(4):
        gsb = lanes([gs_r[2 * ib], gs_r[2 * ib + 1]]).astype(F32)
        deltas.append(jnp.sum(gsb * attf[ib], axis=0, keepdims=True))
    delta = lanes(deltas)
    st[0:1, :] = deltas[0]
    for ib in range(4):
        st[ib : ib + 1, :] = deltas[ib]

    def ds_ex(t, p):
        return copy_to(d_s.at[t, p], d_r.at[t, me], d_ss.at[t, p], d_rs.at[t, me], seq_dev(p))

    def out_block(t, p):
        @pl.when(p != me)
        def _():
            ds_ex(t, p).start()

        @pl.when(p == me)
        def _():
            d_r[t, me] = d_s[t, me]

    def backward(jb):
        rows = pl.ds(pl.multiple_of(256 * jb, 256), 256)
        vb = vn[rows, :]
        kb = lanes([qkv_r[0, 2 * jb], qkv_r[0, 2 * jb + 1]])
        dk = jnp.zeros((HD, 256), F32)
        dv = jnp.zeros((HD, 256), F32)
        for ib in range(4):
            gsb = lanes([gs_r[2 * ib], gs_r[2 * ib + 1]])
            dp = dot(vb, gsb)
            p = ex[ib, rows, :] * itot[ib]
            ds = (p * (dp - st[ib : ib + 1, :])).astype(BF)
            dv = dv + dot_nt(gsb, p.astype(BF))
            dk = dk + dot_nt(pair(qkv_r, 1, ib), ds)
            dqa[:, 256 * ib : 256 * ib + 256] += dot(kb, ds)
        dkb = (dk * SCALE).astype(BF)
        dvb = dv.astype(BF)
        for half in range(2):
            p = 2 * jb + half
            d_s[0, p] = dkb[:, 128 * half : 128 * half + 128]
            d_s[1, p] = dvb[:, 128 * half : 128 * half + 128]
            out_block(0, p)
            out_block(1, p)

    loop(0, 4, backward)
    dq_all = (dqa[...] * SCALE).astype(BF)
    for p in range(8):
        d_s[2, p] = dq_all[:, 128 * p : 128 * p + 128]

    def d_all(t):
        return d_s.at[t], d_r.at[t], d_ss.at[t], d_rs.at[t]

    for t in range(3):
        owe(f"d_r{t}", lambda t=t: recv_all(*d_all(t)))
        owe(f"d_s{t}", lambda t=t: sent_all(*d_all(t)))

    paid("ys_r")
    acc = gp[y].astype(F32)
    for r in range(1, 4):
        acc = acc + yb[lax.rem(y + r, 4)].astype(F32)
    zs[...] = acc.astype(BF).reshape(2, 48, W5)
    owner = lax.div(zl, 2) == c

    def zsend(kk):
        r = lax.rem(zl - (2 * c + kk) + 4, 4)
        step = 4 * lax.div(r, 3) - r
        return r, copy_to(zs.at[kk], zb.at[r], z_ss.at[kk], z_rs.at[r], z_dev(step))

    for kk in range(2):
        r, cp = zsend(kk)

        @pl.when(r != 0)
        def _():
            cp.start()

    def zs_sent():
        for kk in range(2):
            r, cp = zsend(kk)

            @pl.when(r != 0)
            def _():
                cp.wait_send()

    owe("zs_s", zs_sent)

    def mx():
        return copy_to(ms, mb, m_ss, m_rs, seq_dev(lax.rem(me + 4, 8)))

    def fx(xx, cc):
        return copy_to(fs.at[cc], ob.at[x], f_ss.at[cc, xx], f_rs.at[x], xc_dev(xx, cc))

    def fx_recv(xx):
        return copy_to(fs.at[c], ob.at[xx], f_ss.at[c, xx], f_rs.at[xx], xc_dev(xx, c))

    def zs_recv():
        for r, step in ((1, 1), (2, 2), (3, -1)):
            copy_to(zs.at[0], zb.at[r], z_ss.at[0], z_rs.at[r], z_dev(step)).wait_recv()

    paid("zs_s")

    @pl.when(jnp.logical_not(owner))
    def _():
        loop(0, 8, lambda p: out_block(2, p))

    @pl.when(owner)
    def _():
        for r, step in ((1, 1), (2, 2), (3, -1)):
            copy_to(zs.at[0], zb.at[r], z_ss.at[0], z_rs.at[r], z_dev(step)).wait_recv()
        tot = zs[lax.rem(zl, 2)].astype(F32)
        for r in range(1, 4):
            tot = tot + zb[r].astype(F32)
        ms[...] = tot.astype(BF)
        mx().start()
        loop(0, 8, lambda p: out_block(2, p))
        mx().wait_recv()
        norm = 1.0 / jnp.sqrt(F32(32 * 1024))
        both = (ms[...].astype(F32) + mb[...].astype(F32)) * norm
        fs[...] = both.reshape(2, 24, W5).astype(BF)
        loop(0, 4, lambda xx: fx(xx, oc).start())
        loop(1, 4, lambda r: fx(lax.rem(x + r, 4), c).start())
        ob[x] = fs[c]

    def own_sent():
        @pl.when(owner)
        def _():
            mx().wait_send()
            loop(0, 4, lambda xx: fx(xx, oc).wait_send())
            loop(1, 4, lambda r: fx(lax.rem(x + r, 4), c).wait_send())

    owe("own_s", own_sent)

    for t, out, there in ((0, dk_out, dk_hbm), (1, dv_out, dv_hbm), (2, dq_out, dq_hbm)):
        paid(f"d_r{t}")
        out[...] = tr(d_r[t].reshape(CH, ROWS)).astype(BF)
        store(1 + t, out, there)

    loop(1, 4, lambda r: fx_recv(lax.rem(x + r, 4)).wait_recv())

    @pl.when(jnp.logical_not(owner))
    def _():
        fx_recv(x).wait_recv()

    for a in range(TAPS):
        gw_out[a] = lanes([ob[b, :, QC * a : QC * a + QC].astype(F32) for b in range(4)])

    store(4, gw_out, gw_hbm)

    finish()


def hand_over(*refs):
    ins, outs, held, sem = refs[:5], refs[5:10], refs[10:15], refs[15]
    reads = [pltpu.make_async_copy(ins[i], held[i], sem.at[0, i]) for i in range(5)]
    writes = [pltpu.make_async_copy(held[i], outs[i], sem.at[1, i]) for i in range(5)]
    for read in reads:
        read.start()
    for read, write in zip(reads, writes):
        read.wait()
        write.start()
    for write in writes:
        write.wait()


def body(stream_in, queries, key_rows, value_rows, conv_weight, cotangent):
    nat = jax.ShapeDtypeStruct((ROWS, CH), BF)
    V = pltpu.VMEM
    blk = (8, HD, ROWS)
    scratch = [V((ROWS, CH), BF) for _ in range(4)] + [
        V((TAPS, 24, CH), F32),
    ] + [V((ROWS, CH), BF) for _ in range(5)] + [
        V((TAPS, 24, CH), BF),
        V((3,) + blk, BF), V((3,) + blk, BF),
        V((1024, HD), BF), V((1024, HD), BF),
        V((1024, 256), F32), V((4, 1024, 256), F32), V((4, 1, 256), F32), V((4, HD, 256), F32),
        V(blk, BF), V(blk, BF),
        V((4, CH, ROWS), BF), V((ROWS, CH), BF), V((2, 4, 96, EXT), BF), V((4, 96, EXT), BF),
        V((2, 4, 4, 24, W5), BF), V((W5, CH), BF),
        V((4, QC, ROWS), BF), V((4, QC, ROWS), BF),
        V((4, QC, ROWS), BF), V((2, 4, QC, ROWS), BF), V((2, W5, EXT), BF),
        V(blk, BF), V(blk, BF), V((HD, 1024), F32), V((3,) + blk, BF), V((3,) + blk, BF),
        V((4, 96, W5), BF), V((4, 96, W5), BF), V((2, 48, W5), BF), V((4, 48, W5), BF),
        V((48, W5), BF), V((48, W5), BF), V((2, 24, W5), BF), V((4, 24, W5), BF),
    ]
    D = pltpu.SemaphoreType.DMA
    sems = [
        D((6,)), D((5,)), D((3, 8)), D((3, 8)), D((8,)), D((8,)), D((8,)), D((8,)), D((3, 8)), D((3, 8)),
        D((4,)), D((4,)), D((4,)), D, D, D,
        D((4,)), D((4,)), D((3,)), D((3,)), D, D,
        D((4,)), D((4,)), D((2, 4)), D((2, 4)), D((4,)), D((4,)), D((2,)), D((4,)), D, D,
        D((2, 4)), D((4,)),
    ]
    hbm = pl.BlockSpec(memory_space=pl.ANY)
    shapes = (nat, nat, nat, nat, jax.ShapeDtypeStruct((TAPS, 24, CH), F32))
    made = pl.pallas_call(
        kernel,
        out_shape=shapes,
        in_specs=[hbm] * 6,
        out_specs=(hbm,) * 5,
        scratch_shapes=scratch + sems,
        compiler_params=pltpu.CompilerParams(
            collective_id=0, has_side_effects=True, vmem_limit_bytes=58 * 1024 * 1024
        ),
    )(stream_in[0], queries[0], key_rows[0], value_rows[0], jnp.transpose(conv_weight, (1, 0, 2)), cotangent[0])
    gs, dq, dk, dv, gw = pl.pallas_call(
        hand_over,
        out_shape=shapes,
        in_specs=[hbm] * 5,
        out_specs=(hbm,) * 5,
        scratch_shapes=[V((ROWS, CH), BF) for _ in range(4)] + [V((TAPS, 24, CH), F32), D((2, 5))],
    )(*made)
    return gs[None], dq[None], dk[None], dv[None], jnp.transpose(gw, (1, 0, 2))


def solution(mesh):
    act = P("dp", "seq", None)
    wsp = P("dp", None, None)
    return jax.shard_map(
        body,
        mesh=mesh,
        in_specs=(act, act, act, act, wsp, act),
        out_specs=(act, act, act, act, wsp),
        check_vma=False,
    )
```

```python
import jax
import jax.numpy as jnp
from jax import lax
from jax.experimental import pallas as pl
from jax.experimental.pallas import tpu as pltpu
from jax.sharding import PartitionSpec as P

HEADS = 8
HD = 96
TAPS = 5
ROWS = 128
CH = 768
QC = 192
W5 = TAPS * QC
EXT = 640
MESH = pl.DeviceIdType.MESH
F32 = jnp.float32
BF = jnp.bfloat16
NT = (((1,), (1,)), ((), ()))
SCALE = HD ** (-0.5)
LOG2E = 1.4426950408889634
GC = 0.7978845608028654
GA = 0.044715


def dot(a, b):
    return jnp.dot(a, b, preferred_element_type=F32)


def dot_nt(a, b):
    return lax.dot_general(a, b, NT, preferred_element_type=F32)


def lanes(parts):
    return jnp.concatenate(parts, axis=1)


def tr(value):
    return value.astype(F32).T


def copy_to(src, dst, send, recv, dev):
    return pltpu.make_async_remote_copy(
        src_ref=src, dst_ref=dst, send_sem=send, recv_sem=recv, device_id=dev, device_id_type=MESH
    )


def kernel(
    x_in, q_in, k_in, v_in, w_in, c_in,
    gs_hbm, dq_hbm, dk_hbm, dv_hbm, gw_hbm,
    gs_out, dq_out, dk_out, dv_out, gw_out,
    x_ref, q_ref, k_ref, v_ref, c_ref, w_ref,
    qkv_s, qkv_r, kn, vn, st, ex, itot, attf, att_s, att_r,
    cblk, hal, cfull, coth, wbuf, wt, bk_s, bk_r, h_s, h_r, hw,
    gs_s, gs_r, dqa, d_s, d_r, gp, yb, zs, zb, ms, mb, fs, ob,
    in_sem, out_sem, qkv_ss, qkv_rs, att_ss, att_rs, gs_ss, gs_rs, d_ss, d_rs,
    c_ss, c_rs, hal_ss, hal_rs, co_ss, co_rs,
    wy_ss, wy_rs, wz_ss, wz_rs, wc_ss, wc_rs,
    bk_ss, bk_rs, h_ss, h_rs, y_ss, y_rs, z_ss, z_rs, m_ss, m_rs, f_ss, f_rs,
):
    me = lax.axis_index("seq")
    dd = lax.axis_index("dp")
    zh = lax.div(me, 4)
    x = lax.rem(me, 4)
    y = lax.div(dd, 8)
    zl = lax.rem(lax.div(dd, 2), 4)
    c = lax.rem(dd, 2)
    oc = 1 - c
    z = zh * 4 + zl
    odp = y * 8 + zl * 2 + oc

    def seq_dev(p):
        return {"seq": p, "dp": dd}

    def xc_dev(xx, cc):
        return {"seq": zh * 4 + xx, "dp": y * 8 + zl * 2 + cc}

    def y_dev(yy):
        return {"seq": me, "dp": yy * 8 + zl * 2 + c}

    def z_dev(step):
        zz = lax.rem(z + step + 8, 8)
        return {"seq": lax.div(zz, 4) * 4 + x, "dp": y * 8 + lax.rem(zz, 4) * 2 + c}

    def loop(lo, hi, fn):
        def step(i, carry):
            fn(i)
            return carry

        lax.fori_loop(lo, hi, step, 0)

    todo = {}

    def owe(name, fn):
        todo[name] = fn

    def paid(name):
        todo.pop(name)()

    def finish():
        for fn in list(todo.values()):
            fn()

    def store(i, src, dst):
        save = pltpu.make_async_copy(src, dst, out_sem.at[i])
        save.start()
        owe(f"out{i}", save.wait)

    hal[...] = jnp.zeros_like(hal)
    barrier = pltpu.get_barrier_semaphore()

    def hello(dev):
        pl.semaphore_signal(barrier, inc=1, device_id=dev, device_id_type=MESH)

    loop(1, 8, lambda r: hello(seq_dev(lax.rem(me + r, 8))))
    loop(0, 4, lambda xx: hello(xc_dev(xx, oc)))
    loop(1, 4, lambda r: hello(y_dev(lax.rem(y + r, 4))))
    for step in (1, -1, 2, -2):
        hello(z_dev(step))

    loads = []
    for i, (src, dst) in enumerate(((k_in, k_ref), (q_in, q_ref), (v_in, v_ref), (c_in, c_ref), (x_in, x_ref), (w_in, w_ref))):
        load = pltpu.make_async_copy(src, dst, in_sem.at[i])
        load.start()
        loads.append(load)
    owe("x_in", loads[4].wait)
    for i, ref in enumerate((k_ref, q_ref, v_ref)):
        loads[i].wait()
        qkv_s[i] = tr(ref[...]).astype(BF).reshape(8, HD, ROWS)
    loads[5].wait()
    for xs in range(4):

        @pl.when(x == xs)
        def _():
            wbuf[c, y, zl] = lanes([w_ref[a, :, QC * xs : QC * xs + QC] for a in range(TAPS)])

    pl.semaphore_wait(barrier, 18)

    def exch(src, dst, ssem, rsem, p):
        return copy_to(src.at[p], dst.at[me], ssem.at[p], rsem.at[me], seq_dev(p))

    def exch_recv(src, dst, ssem, rsem, p):
        return copy_to(src.at[p], dst.at[p], ssem.at[p], rsem.at[p], seq_dev(p))

    def start_all(src, dst, ssem, rsem):
        loop(1, 8, lambda r: exch(src, dst, ssem, rsem, lax.rem(me + r, 8)).start())

    def recv_all(src, dst, ssem, rsem):
        loop(1, 8, lambda r: exch_recv(src, dst, ssem, rsem, lax.rem(me + r, 8)).wait_recv())

    def sent_all(src, dst, ssem, rsem):
        loop(1, 8, lambda r: exch_recv(src, dst, ssem, rsem, lax.rem(me + r, 8)).wait_send())

    def qkv(t):
        return qkv_s.at[t], qkv_r.at[t], qkv_ss.at[t], qkv_rs.at[t]

    far = 2 - 4 * c

    def wz(i, step, slot):
        return copy_to(wbuf.at[c, y, slot], wbuf.at[c, y, slot], wz_ss.at[i], wz_rs.at[i], z_dev(step))

    def wz_recv(i, step):
        wz(i, step, lax.rem(zl + step + 4, 4)).wait_recv()

    def wz_recv_all():
        wz_recv(0, -1)
        wz_recv(1, 1)
        wz_recv(2, -far)

    def wz_sent_all():
        wz(0, 1, zl).wait_send()
        wz(1, -1, zl).wait_send()
        wz(2, far, zl).wait_send()

    def start_qkv(t):
        start_all(*qkv(t))
        owe(f"qkv_r{t}", lambda: recv_all(*qkv(t)))
        owe(f"qkv_s{t}", lambda: sent_all(*qkv(t)))

    start_qkv(0)
    wz(0, 1, zl).start()
    wz(1, -1, zl).start()
    wz(2, far, zl).start()
    owe("wz_r", wz_recv_all)
    owe("wz_s", wz_sent_all)
    paid("wz_r")

    def wy(yy, slot):
        return copy_to(wbuf.at[c, slot], wbuf.at[c, slot], wy_ss.at[yy], wy_rs.at[slot], y_dev(yy))

    loop(1, 4, lambda r: wy(lax.rem(y + r, 4), y).start())
    owe("wy_r", lambda: loop(1, 4, lambda r: wy(lax.rem(y + r, 4), lax.rem(y + r, 4)).wait_recv()))
    owe("wy_s", lambda: loop(1, 4, lambda r: wy(lax.rem(y + r, 4), y).wait_send()))

    start_qkv(1)
    start_qkv(2)
    loads[3].wait()
    cblk[x] = tr(c_ref[...]).astype(BF)
    for t in range(3):
        qkv_r[t, me] = qkv_s[t, me]
    def cx(xx, slot):
        return copy_to(cblk.at[slot], cblk.at[slot], c_ss.at[xx], c_rs.at[slot], xc_dev(xx, c))

    loop(1, 4, lambda r: cx(lax.rem(x + r, 4), x).start())
    owe("cx_r", lambda: loop(1, 4, lambda r: cx(lax.rem(x + r, 4), lax.rem(x + r, 4)).wait_recv()))
    owe("cx_s", lambda: loop(1, 4, lambda r: cx(lax.rem(x + r, 4), x).wait_send()))

    def edge(p, lo):
        rows = pl.ds(lo, 16)

        return copy_to(c_ref.at[rows], hal.at[pl.ds(lo, 16)], hal_ss.at[lax.rem(p, 4)], hal_rs, seq_dev(p))

    first = jnp.logical_and(zh == 1, x == 0)
    last = jnp.logical_and(zh == 0, x == 3)

    @pl.when(first)
    def _():
        loop(0, 4, lambda p: edge(p, 0).start())

    @pl.when(last)
    def _():
        loop(4, 8, lambda p: edge(p, 112).start())

    def edge_recv():
        @pl.when(zh == 0)
        def _():
            edge(0, 0).wait_recv()

        @pl.when(zh == 1)
        def _():
            edge(0, 112).wait_recv()

    def edge_sent():
        @pl.when(first)
        def _():
            loop(0, 4, lambda p: edge(p, 0).wait_send())

        @pl.when(last)
        def _():
            loop(4, 8, lambda p: edge(p, 112).wait_send())

    owe("edge_r", edge_recv)
    owe("edge_s", edge_sent)
    paid("qkv_r0")
    for b in range(8):
        kn[128 * b : 128 * b + 128, :] = tr(qkv_r[0, b]).astype(BF)
    paid("qkv_r1")

    paid("qkv_r2")
    for b in range(8):
        vn[128 * b : 128 * b + 128, :] = tr(qkv_r[2, b]).astype(BF)

    def pair(ref, t, i):
        return lanes([ref[t, 2 * i], ref[t, 2 * i + 1]])

    def forward(ib):
        qb = lanes([qkv_r[1, 2 * ib], qkv_r[1, 2 * ib + 1]])
        top = None
        for jb in range(4):
            s = dot(kn[256 * jb : 256 * jb + 256, :], qb)
            st[256 * jb : 256 * jb + 256, :] = s
            m = jnp.max(s, axis=0, keepdims=True)
            top = m if top is None else jnp.maximum(top, m)
        tot = jnp.zeros((1, 256), F32)
        acc = jnp.zeros((HD, 256), F32)
        for jb in range(4):
            e = jnp.exp2((st[256 * jb : 256 * jb + 256, :] - top) * (SCALE * LOG2E))
            ex[ib, 256 * jb : 256 * jb + 256, :] = e
            tot = tot + jnp.sum(e, axis=0, keepdims=True)
            acc = acc + dot(pair(qkv_r, 2, jb), e.astype(BF))
        inv = 1.0 / tot
        itot[ib] = inv
        att = acc * inv
        attf[ib] = att
        ab = att.astype(BF)
        for half in range(2):
            p = 2 * ib + half
            att_s[p] = ab[:, 128 * half : 128 * half + 128]

            @pl.when(p != me)
            def _():
                exch(att_s, att_r, att_ss, att_rs, p).start()

            @pl.when(p == me)
            def _():
                att_r[me] = att_s[me]

    loop(0, 4, forward)
    owe("att_r", lambda: recv_all(att_s, att_r, att_ss, att_rs))
    owe("att_s", lambda: sent_all(att_s, att_r, att_ss, att_rs))

    paid("wy_r")

    def wc(slot):
        return copy_to(wbuf.at[slot], wbuf.at[slot], wc_ss, wc_rs, xc_dev(x, oc))

    wc(c).start()
    owe("wc_r", lambda: wc(oc).wait_recv())
    owe("wc_s", lambda: wc(c).wait_send())

    paid("cx_r")
    paid("edge_r")
    halt = tr(hal[...]).astype(BF)
    for cc in range(2):
        for yy in range(4):
            lo = 192 * yy + 96 * cc
            for b in range(4):
                cfull[cc, yy, :, 128 * b : 128 * b + 128] = cblk[b, lo : lo + 96, :]
            cfull[cc, yy, :, 512:640] = halt[lo : lo + 96, :]

    co = copy_to(cfull.at[oc], coth, co_ss, co_rs, xc_dev(x, oc))
    co.start()
    owe("co_r", co.wait_recv)
    owe("co_s", co.wait_send)

    paid("wc_r")
    for n in range(8):
        width = min(128, W5 - 128 * n)
        rows = []
        for cc in range(2):
            for yy in range(4):
                for j in range(4):
                    rows.append(wbuf[j % 2, yy, 2 * cc + j // 2, :, 128 * n : 128 * n + width].astype(F32))
        wt[128 * n : 128 * n + width, :] = jnp.concatenate(rows, axis=0).T.astype(BF)

    cot_all = cfull[...].reshape(CH, EXT)
    back_q = None
    for a in range(TAPS):
        part = dot(wt[QC * a : QC * a + QC, :], cot_all)
        shift = (a - 2) % EXT
        if shift:
            part = pltpu.roll(part, shift, 1)
        back_q = part if back_q is None else back_q + part
    back_b = back_q.astype(BF)
    for b in range(4):
        bk_s[b] = back_b[:, 128 * b : 128 * b + 128]
    bk_r[x] = bk_s[x]

    def bk(xx, slot_from, slot_to):
        return copy_to(bk_s.at[slot_from], bk_r.at[slot_to], bk_ss.at[xx], bk_rs.at[slot_to], xc_dev(xx, c))

    def bk_start(r):
        xx = lax.rem(x + r, 4)
        bk(xx, xx, x).start()

    def bk_wait(r):
        xx = lax.rem(x + r, 4)
        bk(xx, xx, xx).wait_recv()

    loop(1, 4, bk_start)
    owe("bk_r", lambda: loop(1, 4, bk_wait))
    owe("bk_s", lambda: loop(1, 4, lambda r: bk(lax.rem(x + r, 4), lax.rem(x + r, 4), x).wait_send()))

    paid("x_in")
    xt = tr(x_ref[...])
    paid("att_r")
    u = (xt + att_r[...].astype(F32).reshape(CH, ROWS)).astype(BF).astype(F32)
    rs = lax.rsqrt(jnp.mean(u * u, axis=0, keepdims=True) + 1e-6)
    nn = u * rs
    th = jnp.tanh(GC * (nn + GA * (nn * nn * nn)))
    hid = (0.5 * nn * (1.0 + th)).astype(BF)
    h_s[...] = hid.reshape(4, QC, ROWS)
    h_r[c, x] = h_s[x]

    def hx(xx, cc):
        return copy_to(h_s.at[xx], h_r.at[c, x], h_ss.at[cc, xx], h_rs.at[c, x], xc_dev(xx, cc))

    def hx_recv(xx, cc):
        return copy_to(h_s.at[xx], h_r.at[cc, xx], h_ss.at[cc, xx], h_rs.at[cc, xx], xc_dev(xx, cc))

    loop(0, 4, lambda xx: hx(xx, oc).start())
    loop(1, 4, lambda r: hx(lax.rem(x + r, 4), c).start())

    def hx_recv_all():
        loop(0, 4, lambda xx: hx_recv(xx, oc).wait_recv())
        loop(1, 4, lambda r: hx_recv(lax.rem(x + r, 4), c).wait_recv())

    def hx_sent_all():
        loop(0, 4, lambda xx: hx(xx, oc).wait_send())
        loop(1, 4, lambda r: hx(lax.rem(x + r, 4), c).wait_send())

    owe("hx_r", hx_recv_all)
    owe("hx_s", hx_sent_all)

    paid("bk_r")
    bk_all = bk_r[...].astype(F32).reshape(CH, ROWS)
    slope = 0.5 * (1.0 + th) + 0.5 * nn * (1.0 - th * th) * (GC * (1.0 + 3.0 * GA * (nn * nn)))
    dn = bk_all * slope
    mean_dn = jnp.sum(dn * nn, axis=0, keepdims=True) * (1.0 / CH)
    du = rs * (dn - nn * mean_dn)
    gst = (cblk[x].astype(F32) + du).astype(BF)
    gs_s[...] = gst.reshape(8, HD, ROWS)
    gs_r[me] = gs_s[me]
    start_all(gs_s, gs_r, gs_ss, gs_rs)
    owe("gs_r", lambda: recv_all(gs_s, gs_r, gs_ss, gs_rs))
    owe("gs_s", lambda: sent_all(gs_s, gs_r, gs_ss, gs_rs))

    gs_out[...] = tr(gst).astype(BF)
    store(0, gs_out, gs_hbm)

    paid("hx_r")
    for cc in range(2):
        hv = lanes([h_r[cc, b] for b in range(4)] + [jnp.zeros((QC, 128), BF)]).astype(F32)
        for a in range(TAPS):
            shift = (2 - a) % EXT
            hw[cc, QC * a : QC * a + QC, :] = (pltpu.roll(hv, shift, 1) if shift else hv).astype(BF)
    paid("co_r")
    own_c = cfull[c].reshape(384, EXT)
    oth_c = coth[...].reshape(384, EXT)
    for lo, hi in ((0, 512), (512, W5)):
        part = dot_nt(own_c, hw[c, lo:hi, :]) + dot_nt(oth_c, hw[oc, lo:hi, :])
        gp[:, :, lo:hi] = part.astype(BF).reshape(4, 96, hi - lo)

    def ys(r):
        yy = lax.rem(y + r, 4)
        return copy_to(gp.at[yy], yb.at[y], y_ss.at[yy], y_rs.at[y], y_dev(yy))

    def ys_recv(r):
        yy = lax.rem(y + r, 4)
        return copy_to(gp.at[yy], yb.at[yy], y_ss.at[yy], y_rs.at[yy], y_dev(yy))

    loop(1, 4, lambda r: ys(r).start())
    owe("ys_r", lambda: loop(1, 4, lambda r: ys_recv(r).wait_recv()))
    owe("ys_s", lambda: loop(1, 4, lambda r: ys(r).wait_send()))

    paid("gs_r")
    dqa[...] = jnp.zeros_like(dqa)
    deltas = []
    for ib in range(4):
        gsb = lanes([gs_r[2 * ib], gs_r[2 * ib + 1]]).astype(F32)
        deltas.append(jnp.sum(gsb * attf[ib], axis=0, keepdims=True))
    delta = lanes(deltas)
    st[0:1, :] = deltas[0]
    for ib in range(4):
        st[ib : ib + 1, :] = deltas[ib]

    def ds_ex(t, p):
        return copy_to(d_s.at[t, p], d_r.at[t, me], d_ss.at[t, p], d_rs.at[t, me], seq_dev(p))

    def out_block(t, p):
        @pl.when(p != me)
        def _():
            ds_ex(t, p).start()

        @pl.when(p == me)
        def _():
            d_r[t, me] = d_s[t, me]

    def backward(jb):
        rows = pl.ds(pl.multiple_of(256 * jb, 256), 256)
        vb = vn[rows, :]
        kb = lanes([qkv_r[0, 2 * jb], qkv_r[0, 2 * jb + 1]])
        dk = jnp.zeros((HD, 256), F32)
        dv = jnp.zeros((HD, 256), F32)
        for ib in range(4):
            gsb = lanes([gs_r[2 * ib], gs_r[2 * ib + 1]])
            dp = dot(vb, gsb)
            p = ex[ib, rows, :] * itot[ib]
            ds = (p * (dp - st[ib : ib + 1, :])).astype(BF)
            dv = dv + dot_nt(gsb, p.astype(BF))
            dk = dk + dot_nt(pair(qkv_r, 1, ib), ds)
            dqa[:, 256 * ib : 256 * ib + 256] += dot(kb, ds)
        dkb = (dk * SCALE).astype(BF)
        dvb = dv.astype(BF)
        for half in range(2):
            p = 2 * jb + half
            d_s[0, p] = dkb[:, 128 * half : 128 * half + 128]
            d_s[1, p] = dvb[:, 128 * half : 128 * half + 128]
            out_block(0, p)
            out_block(1, p)

    loop(0, 4, backward)
    dq_all = (dqa[...] * SCALE).astype(BF)
    for p in range(8):
        d_s[2, p] = dq_all[:, 128 * p : 128 * p + 128]

    def d_all(t):
        return d_s.at[t], d_r.at[t], d_ss.at[t], d_rs.at[t]

    for t in range(3):
        owe(f"d_r{t}", lambda t=t: recv_all(*d_all(t)))
        owe(f"d_s{t}", lambda t=t: sent_all(*d_all(t)))

    paid("ys_r")
    acc = gp[y].astype(F32)
    for r in range(1, 4):
        acc = acc + yb[lax.rem(y + r, 4)].astype(F32)
    zs[...] = acc.astype(BF).reshape(2, 48, W5)
    owner = lax.div(zl, 2) == c

    def zsend(kk):
        r = lax.rem(zl - (2 * c + kk) + 4, 4)
        step = 4 * lax.div(r, 3) - r
        return r, copy_to(zs.at[kk], zb.at[r], z_ss.at[kk], z_rs.at[r], z_dev(step))

    for kk in range(2):
        r, cp = zsend(kk)

        @pl.when(r != 0)
        def _():
            cp.start()

    def zs_sent():
        for kk in range(2):
            r, cp = zsend(kk)

            @pl.when(r != 0)
            def _():
                cp.wait_send()

    owe("zs_s", zs_sent)

    def mx(cc):
        return copy_to(ms.at[cc], mb.at[cc], m_ss.at[cc], m_rs.at[cc], seq_dev(lax.rem(me + 4, 8)))

    def fx(xx, cc):
        return copy_to(fs.at[cc], ob.at[x], f_ss.at[cc, xx], f_rs.at[x], xc_dev(xx, cc))

    def fx_recv(xx):
        return copy_to(fs.at[c], ob.at[xx], f_ss.at[c, xx], f_rs.at[xx], xc_dev(xx, c))

    def zs_recv():
        for r, step in ((1, 1), (2, 2), (3, -1)):
            copy_to(zs.at[0], zb.at[r], z_ss.at[0], z_rs.at[r], z_dev(step)).wait_recv()

    paid("zs_s")

    @pl.when(jnp.logical_not(owner))
    def _():
        loop(0, 8, lambda p: out_block(2, p))

    @pl.when(owner)
    def _():
        for r, step in ((1, 1), (2, 2), (3, -1)):
            copy_to(zs.at[0], zb.at[r], z_ss.at[0], z_rs.at[r], z_dev(step)).wait_recv()
        tot = zs[lax.rem(zl, 2)].astype(F32)
        for r in range(1, 4):
            tot = tot + zb[r].astype(F32)
        ms[...] = tot.reshape(2, 24, W5).astype(BF)
        mx(0).start()
        mx(1).start()
        loop(0, 8, lambda p: out_block(2, p))
        norm = 1.0 / jnp.sqrt(F32(32 * 1024))
        for cc in range(2):
            mx(cc).wait_recv()
            fs[cc] = ((ms[cc].astype(F32) + mb[cc].astype(F32)) * norm).astype(BF)
            loop(1, 4, lambda r: fx(lax.rem(x + r, 4), cc).start())
            pl.when(cc != c)(fx(x, cc).start)

            @pl.when(cc == c)
            def _():
                ob[x] = fs[cc]

    def own_sent():
        @pl.when(owner)
        def _():
            mx(0).wait_send()
            mx(1).wait_send()
            loop(0, 4, lambda xx: fx(xx, oc).wait_send())
            loop(1, 4, lambda r: fx(lax.rem(x + r, 4), c).wait_send())

    owe("own_s", own_sent)

    for t, out, there in ((0, dk_out, dk_hbm), (1, dv_out, dv_hbm), (2, dq_out, dq_hbm)):
        paid(f"d_r{t}")
        out[...] = tr(d_r[t].reshape(CH, ROWS)).astype(BF)
        store(1 + t, out, there)

    loop(1, 4, lambda r: fx_recv(lax.rem(x + r, 4)).wait_recv())

    @pl.when(jnp.logical_not(owner))
    def _():
        fx_recv(x).wait_recv()

    for a in range(TAPS):
        gw_out[a] = lanes([ob[b, :, QC * a : QC * a + QC].astype(F32) for b in range(4)])

    store(4, gw_out, gw_hbm)

    finish()


def hand_over(*refs):
    ins, outs, held, sem = refs[:5], refs[5:10], refs[10:15], refs[15]
    reads = [pltpu.make_async_copy(ins[i], held[i], sem.at[0, i]) for i in range(5)]
    writes = [pltpu.make_async_copy(held[i], outs[i], sem.at[1, i]) for i in range(5)]
    for read in reads:
        read.start()
    for read, write in zip(reads, writes):
        read.wait()
        write.start()
    for write in writes:
        write.wait()


def body(stream_in, queries, key_rows, value_rows, conv_weight, cotangent):
    nat = jax.ShapeDtypeStruct((ROWS, CH), BF)
    V = pltpu.VMEM
    blk = (8, HD, ROWS)
    scratch = [V((ROWS, CH), BF) for _ in range(4)] + [
        V((TAPS, 24, CH), F32),
    ] + [V((ROWS, CH), BF) for _ in range(5)] + [
        V((TAPS, 24, CH), BF),
        V((3,) + blk, BF), V((3,) + blk, BF),
        V((1024, HD), BF), V((1024, HD), BF),
        V((1024, 256), F32), V((4, 1024, 256), F32), V((4, 1, 256), F32), V((4, HD, 256), F32),
        V(blk, BF), V(blk, BF),
        V((4, CH, ROWS), BF), V((ROWS, CH), BF), V((2, 4, 96, EXT), BF), V((4, 96, EXT), BF),
        V((2, 4, 4, 24, W5), BF), V((W5, CH), BF),
        V((4, QC, ROWS), BF), V((4, QC, ROWS), BF),
        V((4, QC, ROWS), BF), V((2, 4, QC, ROWS), BF), V((2, W5, EXT), BF),
        V(blk, BF), V(blk, BF), V((HD, 1024), F32), V((3,) + blk, BF), V((3,) + blk, BF),
        V((4, 96, W5), BF), V((4, 96, W5), BF), V((2, 48, W5), BF), V((4, 48, W5), BF),
        V((2, 24, W5), BF), V((2, 24, W5), BF), V((2, 24, W5), BF), V((4, 24, W5), BF),
    ]
    D = pltpu.SemaphoreType.DMA
    sems = [
        D((6,)), D((5,)), D((3, 8)), D((3, 8)), D((8,)), D((8,)), D((8,)), D((8,)), D((3, 8)), D((3, 8)),
        D((4,)), D((4,)), D((4,)), D, D, D,
        D((4,)), D((4,)), D((3,)), D((3,)), D, D,
        D((4,)), D((4,)), D((2, 4)), D((2, 4)), D((4,)), D((4,)), D((2,)), D((4,)), D((2,)), D((2,)),
        D((2, 4)), D((4,)),
    ]
    hbm = pl.BlockSpec(memory_space=pl.ANY)
    shapes = (nat, nat, nat, nat, jax.ShapeDtypeStruct((TAPS, 24, CH), F32))
    made = pl.pallas_call(
        kernel,
        out_shape=shapes,
        in_specs=[hbm] * 6,
        out_specs=(hbm,) * 5,
        scratch_shapes=scratch + sems,
        compiler_params=pltpu.CompilerParams(
            collective_id=0, has_side_effects=True, vmem_limit_bytes=58 * 1024 * 1024
        ),
    )(stream_in[0], queries[0], key_rows[0], value_rows[0], jnp.transpose(conv_weight, (1, 0, 2)), cotangent[0])
    gs, dq, dk, dv, gw = pl.pallas_call(
        hand_over,
        out_shape=shapes,
        in_specs=[hbm] * 5,
        out_specs=(hbm,) * 5,
        scratch_shapes=[V((ROWS, CH), BF) for _ in range(4)] + [V((TAPS, 24, CH), F32), D((2, 5))],
    )(*made)
    return gs[None], dq[None], dk[None], dv[None], jnp.transpose(gw, (1, 0, 2))


def solution(mesh):
    act = P("dp", "seq", None)
    wsp = P("dp", None, None)
    return jax.shard_map(
        body,
        mesh=mesh,
        in_specs=(act, act, act, act, wsp, act),
        out_specs=(act, act, act, act, wsp),
        check_vma=False,
    )
```
